32 devices in a mesh: slab: 4 (over z), bulk: 8 (over y, x, core).
Axes of the slice: x: 2, y: 2, z: 4, core: 2. Of those that a mesh axis runs over, the one named last changes fastest.
Arguments:
- atom_counts: int32 [16, 64, 1024], P('slab', 'bulk'), may hold values from 0 to 15
- ion_flags: int32 [16, 64, 1024], P(None, 'bulk', 'slab'), may hold values 0 or 1
- charge_cells: int32 [32768], P(('slab', 'bulk')), may hold values from 0 to 32767
- charge_values: float32 [32768], P(('slab', 'bulk')), may hold values from -16 to 16
Outputs:
- potential: float32 [16, 64, 1024], P(None, 'bulk', 'slab')
- misfit: float32 [16, 64, 1024], P(None, 'bulk', 'slab')
The draws below stay inside these ranges and needn't reach their ends.
Inputs may be any that keep to these rules, and one draw needn't show every extreme that they name: Entry i of charge_cells is the flat index z * 8 * 256 + x * 256 + y of a cell in the brick of the device that holds entry i; cells may repeat.
All inputs are finite; a program needn't handle non-finite values. No bound on the sum of `ion_flags` on one device may be relied on, other than what follows from the above.
Results may differ from the reference program's by a relative error of at most 0.0001.
Values sent between devices are 32-bit elements; how exact they have to be, the bound alone decides.
A program may use at most 128 MiB of HBM per device.

```python
import math
import jax
import jax.numpy as jnp
import numpy as np
from jax import lax

CX = 8
CYB = 256
Q = 1024
GRID_LEVEL_COUNT = 4
SWEEPS = 1
COARSE = 8
NEWTON = 2
NZ = 16
NX = 64
NY = 1024
CHARGES = 32768
N_BULK = 8


def place_ends(array, stream_key, low, top_value):
    index_at = [jax.random.randint(jax.random.fold_in(stream_key, axis), (), 0, length) for axis, length in enumerate(array.shape)]
    main_axis = array.shape.index(max(array.shape))
    next_to = index_at[:main_axis] + [(index_at[main_axis] + 1) % array.shape[main_axis]] + index_at[main_axis + 1:]
    return array.at[tuple(index_at)].set(low).at[tuple(next_to)].set(top_value)


def block_scale(own_key, shape, cuts, low, high):
    def one(dim, parts):
        draws = jax.random.uniform(jax.random.fold_in(jax.random.fold_in(own_key, 6), dim), (parts,), jnp.float32, low / len(cuts), high / len(cuts))
        return jnp.repeat(jnp.exp(draws), shape[dim] // parts).reshape((-1,) + (1,) * (len(shape) - dim - 1))

    factor_of = one(*cuts[0])
    for cut in cuts[1:]:
        factor_of = factor_of * one(*cut)
    return factor_of


def rank_table(number_of, lean):
    loads = [(1 << 20) // math.isqrt(rank ** lean) + 1 for rank in range(1, number_of + 1)]
    spread = 1 + sum(loads) // (1 << 30)
    return np.cumsum(np.array([max(1, weight // spread) for weight in loads]))


def ranked_ids(own_key, shape, number_of, slope):
    listing = rank_table(number_of, slope)
    pick = jax.random.randint(jax.random.fold_in(own_key, 1), shape, 0, int(listing[number_of - 1]))
    standing = jnp.searchsorted(jnp.asarray(listing, jnp.int32), pick, side="right")
    return jax.random.permutation(jax.random.fold_in(own_key, 2), number_of)[standing].astype(jnp.int32)


def normal_values(key, dims, scale, bound, split=(), held_as=jnp.bfloat16):
    drawn = scale * jax.random.normal(key, dims, jnp.float32)
    if split:
        drawn = drawn * block_scale(key, dims, split, -0.22, 0.18)
    return jnp.clip(drawn, -bound, bound).astype(held_as)


def setup_inputs(seed: int = 0) -> dict:
    splits = jax.random.split(jax.random.key(seed), 5)
    return {
        "atom_counts": place_ends(ranked_ids(splits[0], (NZ, NX, NY), 16, 2), jax.random.fold_in(splits[0], 3), 0, 15).astype(jnp.int32),
        "ion_flags": place_ends((jax.random.randint(splits[1], (NZ, NX, NY), 0, 4) < 1).astype(jnp.int32), jax.random.fold_in(splits[1], 1), 0, 1),
        "charge_cells": place_ends(jax.random.randint(splits[2], (CHARGES,), 0, NZ * CX * CYB), jax.random.fold_in(splits[2], 1), 0, (NZ * CX * CYB) - 1).astype(jnp.int32),
        "charge_values": normal_values(splits[3], (CHARGES,), 4.0, 16.0, ((0, 32),), jnp.float32),
    }


taper_raw = np.exp(-0.5 * (np.arange(-4, 5) / 1.5) ** 2)
taper_weights = taper_raw / taper_raw.sum()
damping = 0.8
screening = 1.0
density_scale = 2.0


def taper_sum(padded, dimension):
    length = padded.shape[dimension] - 8
    summed = float(taper_weights[0]) * lax.slice_in_dim(padded, 0, length, axis=dimension)
    for offset in range(1, 9):
        summed = summed + float(taper_weights[offset]) * lax.slice_in_dim(padded, offset, offset + length, axis=dimension)
    return summed


def smooth_along(values_in, dimension):
    widths = [(0, 0), (0, 0), (0, 0)]
    widths[dimension] = (4, 4)
    return taper_sum(jnp.pad(values_in, widths), dimension)


def shifted(padded, dimension, offset):
    starts = [1, 1, 1]
    starts[dimension] = 1 + offset
    limits = [starts[0] + padded.shape[0] - 2, starts[1] + padded.shape[1] - 2, starts[2] + padded.shape[2] - 2]
    return lax.slice(padded, starts, limits)


def laplace_part(field_pad, dielectric_pad, scaling):
    middle = shifted(field_pad, 0, 0)
    dielectric_mid = shifted(dielectric_pad, 0, 0)
    summed = jnp.zeros_like(middle)
    for dimension in range(3):
        for offset in (-1, 1):
            weight_face = 0.5 * (dielectric_mid + shifted(dielectric_pad, dimension, offset))
            summed = summed + weight_face * (middle - shifted(field_pad, dimension, offset))
    return scaling * summed


def total_face_weight(dielectric_pad, scaling):
    dielectric_mid = shifted(dielectric_pad, 0, 0)
    summed = jnp.zeros_like(dielectric_mid)
    for dimension in range(3):
        for offset in (-1, 1):
            summed = summed + 0.5 * (dielectric_mid + shifted(dielectric_pad, dimension, offset))
    return scaling * summed


def coarsen(values_in):
    sizes_in = values_in.shape
    blocks = values_in.reshape(sizes_in[0] // 2, 2, sizes_in[1] // 2, 2, sizes_in[2] // 2, 2)
    return blocks.sum(axis=(1, 3, 5)) * 0.125


def refine(coarse):
    return jnp.repeat(jnp.repeat(jnp.repeat(coarse, 2, axis=0), 2, axis=1), 2, axis=2)


def multigrid(grid_height, target, level_list):
    dielectric_pad, reaction, diagonal, scaling = level_list[grid_height]

    def operate(iterate):
        return laplace_part(jnp.pad(iterate, 1), dielectric_pad, scaling) + reaction * iterate

    deepest = grid_height == len(level_list) - 1
    iterate = damping * target / diagonal
    repeats = COARSE - 1 if deepest else SWEEPS - 1
    for repeat in range(repeats):
        iterate = iterate + damping * (target - operate(iterate)) / diagonal
    if deepest:
        return iterate
    residue = target - operate(iterate)
    iterate = iterate + refine(multigrid(grid_height + 1, coarsen(residue), level_list))
    for repeat in range(SWEEPS):
        iterate = iterate + damping * (target - operate(iterate)) / diagonal
    return iterate


def reference(atom_counts, ion_flags, charge_cells, charge_values):
    density = atom_counts.astype(jnp.float32)
    smoothed = smooth_along(smooth_along(smooth_along(density, 2), 0), 1)
    shading = jnp.exp(-smoothed / density_scale)
    dielectric = 2.0 + 78.0 * shading
    reaction_base = screening * shading * shading * (1.0 - ion_flags.astype(jnp.float32))
    serial = jnp.arange(CHARGES, dtype=jnp.int32)
    device = serial // Q
    slab_index = device // N_BULK
    bulk_index = device % N_BULK
    planes = charge_cells // (CX * CYB)
    remainder = charge_cells % (CX * CYB)
    row_index = bulk_index * CX + remainder // CYB
    column = slab_index * CYB + remainder % CYB
    source = jnp.zeros((NZ, NX, NY), jnp.float32).at[planes, row_index, column].add(charge_values)
    dielectrics = [dielectric]
    for grid_height in range(1, GRID_LEVEL_COUNT):
        dielectrics.append(coarsen(dielectrics[-1]))
    scale_factors = [0.25 ** grid_height for grid_height in range(GRID_LEVEL_COUNT)]
    padded_dielectric_maps = [jnp.pad(item, 1) for item in dielectrics]
    summed_face_weights = [total_face_weight(padded_dielectric_maps[grid_height], scale_factors[grid_height]) for grid_height in range(GRID_LEVEL_COUNT)]
    potential = jnp.zeros((NZ, NX, NY), jnp.float32)
    for newton in range(NEWTON):
        misfit = laplace_part(jnp.pad(potential, 1), padded_dielectric_maps[0], 1.0) + reaction_base * jnp.sinh(potential) - source
        reaction_terms = [reaction_base * jnp.cosh(potential)]
        for grid_height in range(1, GRID_LEVEL_COUNT):
            reaction_terms.append(coarsen(reaction_terms[-1]))
        level_list = [(padded_dielectric_maps[grid_height], reaction_terms[grid_height], summed_face_weights[grid_height] + reaction_terms[grid_height], scale_factors[grid_height]) for grid_height in range(GRID_LEVEL_COUNT)]
        potential = potential + multigrid(0, -misfit, level_list)
    misfit = laplace_part(jnp.pad(potential, 1), padded_dielectric_maps[0], 1.0) + reaction_base * jnp.sinh(potential) - source
    return potential, misfit
```

```python
import jax
import jax.numpy as jnp
import numpy as np
from jax import lax
from jax.experimental import pallas as pl
from jax.experimental.pallas import tpu as pltpu
from jax.sharding import PartitionSpec as P

COARSE = 8
NEWTON = 2
H = 4

taper_raw = np.exp(-0.5 * (np.arange(-4, 5) / 1.5) ** 2)
taper_weights = taper_raw / taper_raw.sum()
damping = 0.8
rest = 1.0 - damping
screening = 1.0
density_scale = 2.0

MESH_ID = pl.DeviceIdType.MESH
LN2 = float(np.log(2.0))
f32 = jnp.float32


def iota(shape, dim):
    return lax.broadcasted_iota(jnp.int32, shape, dim)


def log2(n):
    return int(n).bit_length() - 1


def mm(a, b):
    return lax.dot_general(
        a, b, (((1,), (0,)), ((), ())),
        precision=lax.Precision.HIGHEST, preferred_element_type=f32,
    )


def sinh_cosh(p):
    a, b = jnp.exp(p - LN2), jnp.exp(-p - LN2)
    q = jnp.minimum(p * p, 1.0)
    small = p * (
        1.0
        + q * (1 / 6) * (1.0 + q * (1 / 20) * (1.0 + q * (1 / 42) * (1.0 + q * (1 / 72) * (1.0 + q * (1 / 110)))))
    )
    return jnp.where(jnp.abs(p) < 1.0, small, a - b), a + b


def taper_y(density):
    width = density.shape[1]
    lane = iota(density.shape, 1)
    summed = float(taper_weights[4]) * density
    for k in range(1, 5):
        before = jnp.where(lane < k, 0.0, pltpu.roll(density, k, 1))
        after = jnp.where(lane >= width - k, 0.0, pltpu.roll(density, width - k, 1))
        summed = summed + float(taper_weights[4 + k]) * (before + after)
    return summed


def taper_z(rows, z, cx):
    i, j = iota((rows, rows), 0), iota((rows, rows), 1)
    far = jnp.abs((i & (z - 1)) - (j >> log2(cx)))
    band = jnp.zeros((rows, rows), f32)
    for k in range(5):
        band = jnp.where(far == k, float(taper_weights[4 + k]), band)
    return jnp.where((i >> log2(z)) == (j & (cx - 1)), band, 0.0)


def scattered(cells, values, rows, z, cx, y):
    entries = cells.shape[1]
    ly, lx = log2(y), log2(cx)
    row = ((cells >> ly) & (cx - 1)) * z + (cells >> (ly + lx))
    at_row = jnp.where(iota((rows, entries), 0) == row, values, 0.0)
    at_y = jnp.where(iota((y, entries), 0) == (cells & (y - 1)), f32(1.0), f32(0.0))
    return lax.dot_general(
        at_row, at_y, (((1,), (1,)), ((), ())),
        precision=lax.Precision.HIGHEST, preferred_element_type=f32,
    )


def lanes_at(v, index):
    parts = [
        jnp.take_along_axis(v[i : i + 8], index, axis=1, mode="promise_in_bounds")
        for i in range(0, v.shape[0], 8)
    ]
    return parts[0] if len(parts) == 1 else jnp.concatenate(parts, axis=0)


def halved(v, index):
    return lanes_at(v + pltpu.roll(v, 127, 1), index)


def solver(
    slabs, bulks, nz, cx, y,
    atoms_hbm, flags_hbm, cells_hbm, values_hbm, pot_out, mis_out,
    atoms_in, flags_in, cells_in, values_in,
    ay, abuf, dens, opened, src, yh_opened, yh_src,
    d0, rb, wx, wyp, wym, wzp, wzm, face, c0, step0, v0, tgt, pot, pot2, tmp,
    d1, w1x, w1yp, w1ym, w1zp, w1zm, face1, c1, step1, t1, v1, hv1, tmp1, tmp2,
    own0, own1, got0, got1, w2, w3, v2_ref, e_ref, tmp3, turned,
    load_sem, a_send, a_recv, x_send, x_recv, y_send, y_recv,
    v_send, v_recv, g_send, g_recv,
):
    s, b = lax.axis_index("slab"), lax.axis_index("bulk")
    z0, z1, z2, z3 = nz, nz // 2, nz // 4, nz // 8
    X0, X1 = cx + 2 * H, cx // 2 + H
    H1 = H // 2
    W0, W1 = y + 128, y // 2 + 128
    mrows = 2 * z2
    rows2, rows3 = bulks * mrows, bulks * z3
    at_left, at_right = b == 0, b == bulks - 1
    at_low, at_high = s == 0, s == slabs - 1
    has_left, has_right = b > 0, b < bulks - 1
    has_low, has_high = s > 0, s < slabs - 1

    loads = [
        pltpu.make_async_copy(there, here, load_sem.at[i])
        for i, (there, here) in enumerate((
            (atoms_hbm, atoms_in), (cells_hbm, cells_in), (values_hbm, values_in),
            (flags_hbm.at[:, 0:128], flags_in.at[0]), (flags_hbm.at[:, 128:256], flags_in.at[1]),
        ))
    ]
    for load in loads:
        load.start()

    barrier = pltpu.get_barrier_semaphore()
    for k in range(1, slabs):
        pl.semaphore_signal(
            barrier, inc=1, device_id=(lax.rem(s + k, slabs), b), device_id_type=MESH_ID
        )
    for k in range(1, bulks):
        pl.semaphore_signal(
            barrier, inc=1, device_id=(s, lax.rem(b + k, bulks)), device_id_type=MESH_ID
        )

    def clear(*refs):
        for ref in refs:
            ref[...] = jnp.zeros(ref.shape, ref.dtype)

    @pl.when(at_left)
    def _():
        clear(dens.at[0:cx], opened.at[0:H], src.at[0:H], pot.at[0:H], hv1.at[0, 0], hv1.at[1, 0])

    @pl.when(at_right)
    def _():
        clear(
            dens.at[2 * cx : 3 * cx], opened.at[H + cx : X0], src.at[H + cx : X0],
            pot.at[H + cx : X0], hv1.at[0, 1], hv1.at[1, 1],
        )

    @pl.when(at_low)
    def _():
        clear(got0.at[1], got1.at[1], yh_opened.at[0], yh_src.at[0])

    @pl.when(at_high)
    def _():
        clear(got0.at[2], got1.at[2], yh_opened.at[1], yh_src.at[1])

    def remote(source, target, send, recv, to):
        return pltpu.make_async_remote_copy(
            src_ref=source, dst_ref=target, send_sem=send, recv_sem=recv,
            device_id=to, device_id_type=MESH_ID,
        )

    right, left = (s, b + 1), (s, b - 1)
    high, low = (s + 1, b), (s - 1, b)
    sent = []

    def go(copy, can):
        pl.when(can)(copy.start)
        sent.append((copy, can))

    loads[0].wait()
    smooth_y = taper_y(atoms_in[...].astype(f32).reshape(-1, slabs * y))
    arows = smooth_y.shape[0]
    lane_a = iota((arows, 128), 1)
    nothing = jnp.zeros((arows, 128), f32)
    for t in range(slabs):
        ay[t, :, 0:y] = smooth_y[:, t * y : (t + 1) * y]
        after = smooth_y[:, (t + 1) * y : (t + 1) * y + 128] if t < slabs - 1 else nothing
        before = smooth_y[:, t * y - 128 : t * y] if t else nothing
        ay[t, :, y:W0] = jnp.where(lane_a < 64, after, before)
    for load in loads[1:]:
        load.wait()
    charges = scattered(cells_in[...], values_in[...], cx * z0, z0, cx, y)
    for x in range(cx):
        src[H + x, :, 0:y] = charges[x * z0 : (x + 1) * z0]
        for i in range(2):
            flags = flags_in[i, pl.ds(x, nz, stride=cx), :]
            opened[H + x, :, i * 128 : (i + 1) * 128] = 1.0 - flags.astype(f32)

    slab_copies = []
    for k in range(1, slabs):
        to, came = lax.rem(s + k, slabs), lax.rem(s + slabs - k, slabs)
        slab_copies.append([
            remote(ay.at[to], abuf.at[slot], a_send.at[k], a_recv.at[k], (to, b))
            for slot in (s, came)
        ])
    pl.semaphore_wait(barrier, slabs + bulks - 2)
    for out, _ in slab_copies:
        out.start()
    abuf[s] = ay[s]

    y_copies, x_copies = [], []
    for i, (field, halo) in enumerate(((opened, yh_opened), (src, yh_src))):
        y_copies.append((
            remote(field.at[H : H + cx, :, y - 128 : y], halo.at[0], y_send.at[i, 0], y_recv.at[i, 0], high),
            has_high, has_low,
        ))
        y_copies.append((
            remote(field.at[H : H + cx, :, 0:128], halo.at[1], y_send.at[i, 1], y_recv.at[i, 1], low),
            has_low, has_high,
        ))

    def rows_both_ways(source, target, slot, lanes):
        return [
            (remote(
                source.at[cx : cx + H, :, lanes], target.at[0:H, :, lanes],
                x_send.at[slot, 0], x_recv.at[slot, 0], right,
            ), has_right, has_left),
            (remote(
                source.at[H : 2 * H, :, lanes], target.at[H + cx : X0, :, lanes],
                x_send.at[slot, 1], x_recv.at[slot, 1], left,
            ), has_left, has_right),
        ]

    x_copies += rows_both_ways(opened, opened, 0, slice(0, y))
    x_copies += rows_both_ways(src, src, 1, slice(0, y))
    for copy, can, _ in y_copies + x_copies:
        go(copy, can)
    corner_copies = rows_both_ways(opened, opened, 2, slice(y, W0)) + rows_both_ways(src, src, 3, slice(y, W0))

    along_z = taper_z(cx * z0, z0, cx)
    for _, into in slab_copies:
        into.wait_recv()
    smooth_z = mm(along_z, abuf[...].reshape(cx * z0, W0))
    dens[cx : 2 * cx] = smooth_z.reshape(cx, z0, W0)
    dens_copies = [
        (remote(dens.at[cx : 2 * cx], dens.at[0:cx], x_send.at[4, 0], x_recv.at[4, 0], right), has_right, has_left),
        (remote(dens.at[cx : 2 * cx], dens.at[2 * cx : 3 * cx], x_send.at[4, 1], x_recv.at[4, 1], left), has_left, has_right),
    ]
    for copy, can, _ in dens_copies:
        go(copy, can)

    for copy, _, can in y_copies:
        pl.when(can)(copy.wait_recv)
    lane_h = iota((z0, 128), 1)
    for field, halo in ((opened, yh_opened), (src, yh_src)):
        for x in range(cx):
            field[H + x, :, y:W0] = jnp.where(lane_h < 64, halo[1, x], halo[0, x])
    for copy, can, _ in corner_copies:
        go(copy, can)

    lane0 = iota((z0, W0), 1)
    keep_low = jnp.where(at_low, f32(0.0), f32(1.0))
    keep_high = jnp.where(at_high, f32(0.0), f32(1.0))
    keep_y = jnp.where(lane0 < y, 1.0, jnp.where(lane0 < y + 64, keep_high, keep_low))
    keep_left = jnp.where(at_left, f32(0.0), f32(1.0))
    keep_right = jnp.where(at_right, f32(0.0), f32(1.0))
    zrow0 = iota((z0, W0), 0)
    lane128 = iota((8, 128), 1)
    even = (2 * lane128) & 127
    half = lane128 >> 1
    half_up = 64 + half
    half_split = jnp.where(lane128 < 64, half, half_up)

    for copy, _, can in dens_copies:
        pl.when(can)(copy.wait_recv)
    for copy, _, can in x_copies + corner_copies:
        pl.when(can)(copy.wait_recv)
    for x in range(X0):
        smoothed = float(taper_weights[4]) * dens[x + 4]
        for k in range(1, 5):
            smoothed = smoothed + float(taper_weights[4 + k]) * (dens[x + 4 - k] + dens[x + 4 + k])
        shading = jnp.exp(-smoothed / density_scale)
        keep = keep_y
        if x < H:
            keep = keep_y * keep_left
        elif x >= H + cx:
            keep = keep_y * keep_right
        d0[x] = keep * (2.0 + 78.0 * shading)
        rb[x] = screening * shading * shading * opened[x]

    def weights(d, wx, wyp, wym, wzp, wzm, face, scale):
        n, z, w = d.shape
        zrow = iota((z, w), 0)
        for x in range(n):
            if x < n - 1:
                wx[x] = (0.5 * scale) * (d[x] + d[x + 1])
        for x in range(1, n - 1):
            v = d[x]
            yp = (0.5 * scale) * (v + pltpu.roll(v, w - 1, 1))
            ym = (0.5 * scale) * (v + pltpu.roll(v, 1, 1))
            zp = jnp.where(zrow == z - 1, 0.0, (0.5 * scale) * (v + pltpu.roll(v, z - 1, 0)))
            zm = jnp.where(zrow == 0, 0.0, (0.5 * scale) * (v + pltpu.roll(v, 1, 0)))
            wyp[x], wym[x], wzp[x], wzm[x] = yp, ym, zp, zm
            ends = jnp.where((zrow == 0) | (zrow == z - 1), (0.5 * scale) * v, 0.0)
            face[x] = wx[x - 1] + wx[x] + yp + ym + zp + zm + ends

    def around(v, x, wx, wyp, wym, wzp, wzm):
        here = v[x]
        z, w = here.shape
        return (
            (wx[x] * v[x + 1] + wx[x - 1] * v[x - 1])
            + (wzp[x] * pltpu.roll(here, z - 1, 0) + wzm[x] * pltpu.roll(here, 1, 0))
            + (wyp[x] * pltpu.roll(here, w - 1, 1) + wym[x] * pltpu.roll(here, 1, 1))
        )

    level0 = (wx, wyp, wym, wzp, wzm)
    level1 = (w1x, w1yp, w1ym, w1zp, w1zm)

    def coarse_row(a, c, slot):
        both = a + c
        lane = iota((z1, 128), 1)
        parts = []
        for i in range(3):
            tmp[slot, i] = both[:, i * 128 : (i + 1) * 128]
            parts.append(halved(
                tmp[slot, i, pl.ds(0, z1, stride=2), :] + tmp[slot, i, pl.ds(1, z1, stride=2), :], even
            ))
        return 0.125 * jnp.concatenate([jnp.where(lane < 64, parts[0], parts[1]), parts[2]], axis=1)

    def fine_row(c, slot):
        for i, index in enumerate((half, half_up, half_split)):
            wide = lanes_at(c[:, 128 * (i // 2) : 128 * (i // 2) + 128], index)
            tmp[slot, i, pl.ds(0, z1, stride=2), :] = wide
            tmp[slot, i, pl.ds(1, z1, stride=2), :] = wide
        return jnp.concatenate([tmp[slot, i] for i in range(3)], axis=1)

    def message(f, slot):
        for k in range(2):
            tmp1[slot, k * z1 : (k + 1) * z1, :] = f(H1 + 2 * k) + f(H1 + 2 * k + 1)
        w = tmp1[slot, pl.ds(0, mrows, stride=2), :] + tmp1[slot, pl.ds(1, mrows, stride=2), :]
        return 0.125 * halved(w, even)

    def safe_step(d, diagonal):
        return jnp.where(d > 0.0, damping / diagonal, 0.0)

    def gather_send(n, own, got):
        whole = [(own, got.at[0, b], (s, lax.rem(b + k, bulks))) for k in range(1, bulks)]
        for source, target, to in whole:
            remote(source, target, g_send.at[n, 0], g_recv.at[n, 0], to).start()
        for side, can, row in ((1, has_high, s + 1), (2, has_low, s - 1)):
            @pl.when(can)
            def _():
                for k in range(bulks):
                    remote(
                        own, got.at[side, b], g_send.at[n, side], g_recv.at[n, side],
                        (row, lax.rem(b + k, bulks)),
                    ).start()

    def gather_copy(n, got, side):
        part = got.at[0, 0 : bulks - 1] if side == 0 else got.at[side]
        return remote(part, part, g_send.at[n, side], g_recv.at[n, side], (s, lax.rem(b + 1, bulks)))

    def gather_wait(n, got):
        gather_copy(n, got, 0).wait_recv()
        pl.when(has_low)(gather_copy(n, got, 1).wait_recv)
        pl.when(has_high)(gather_copy(n, got, 2).wait_recv)

    def gather_drain(n, got):
        gather_copy(n, got, 0).wait_send()
        pl.when(has_high)(gather_copy(n, got, 1).wait_send)
        pl.when(has_low)(gather_copy(n, got, 2).wait_send)

    def flat_weights(w_ref, d, z, scale):
        rows = d.shape[0]
        row = iota(d.shape, 0)
        zrow = row & (z - 1)
        total = None
        for i, (outside, other) in enumerate((
            (row < z, pltpu.roll(d, z, 0)), (row >= rows - z, pltpu.roll(d, rows - z, 0)),
            (zrow == 0, pltpu.roll(d, 1, 0)), (zrow == z - 1, pltpu.roll(d, rows - 1, 0)),
            (None, pltpu.roll(d, 1, 1)), (None, pltpu.roll(d, 127, 1)),
        )):
            w = (0.5 * scale) * (d + other)
            if outside is None:
                w_ref[i] = w
            else:
                w_ref[i] = jnp.where(outside, 0.0, w)
                w = jnp.where(outside, (0.5 * scale) * d, w)
            total = w if total is None else total + w
        return total

    def flat_around(w_ref, v, z):
        rows = v.shape[0]
        return (
            (w_ref[4] * pltpu.roll(v, 1, 1) + w_ref[5] * pltpu.roll(v, 127, 1))
            + ((w_ref[0] * pltpu.roll(v, z, 0) + w_ref[1] * pltpu.roll(v, rows - z, 0))
               + (w_ref[2] * pltpu.roll(v, 1, 0) + w_ref[3] * pltpu.roll(v, rows - 1, 0)))
        )

    def flat_coarse(v, z, slot):
        rows = v.shape[0]
        tmp3[slot] = v
        w = tmp3[slot, pl.ds(0, rows // 2, stride=2), :] + tmp3[slot, pl.ds(1, rows // 2, stride=2), :]
        zc = z // 2
        pieces = [w[(2 * k) * zc : (2 * k + 1) * zc] + w[(2 * k + 1) * zc : (2 * k + 2) * zc] for k in range(rows // (4 * zc))]
        return 0.125 * halved(jnp.concatenate(pieces, axis=0), even)

    def flat_fine(v, z):
        wide = lanes_at(v, half)
        zc = z // 2
        pieces = []
        for k in range(v.shape[0] // zc):
            pieces += [wide[k * zc : (k + 1) * zc]] * 2
        doubled = jnp.concatenate(pieces, axis=0)
        rows = 4 * v.shape[0]
        tmp3[0, pl.ds(0, rows // 2, stride=2), :] = doubled
        tmp3[0, pl.ds(1, rows // 2, stride=2), :] = doubled
        return tmp3[0]

    weights(d0, *level0, face, 1.0)
    for k in range(X1):
        d1[k] = coarse_row(d0[2 * k], d0[2 * k + 1], k)
    weights(d1, *level1, face1, 0.25)
    face2 = face3 = None
    d2 = None

    for n in range(NEWTON):
        inner = range(1, X0 - 1)
        if n == 0:
            target, c_of = src, rb
        else:
            target, c_of = tgt, c0

            def reaction(x):
                sh, ch = sinh_cosh(pot[x])
                c0[x] = rb[x] * ch
                if x in inner:
                    tgt[x] = src[x] - rb[x] * sh
                    return True

            def misfit_row(x):
                tgt[x] = tgt[x] - face[x] * pot[x] + around(pot, x, *level0)

            mine = range(H, H + cx)
            for x in mine:
                reaction(x)
            for x in mine[1:-1]:
                misfit_row(x)
            for copy, _, can in pot_copies:
                pl.when(can)(copy.wait_recv)
            for x in range(X0):
                if x not in mine:
                    reaction(x)
            for x in inner:
                if x not in mine[1:-1]:
                    misfit_row(x)
        for x in inner:
            st = safe_step(d0[x], face[x] + c_of[x])
            step0[x] = st
            v0[x] = st * target[x]
        for k in range(X1):
            c1[k] = coarse_row(c_of[2 * k], c_of[2 * k + 1], k)

        def residual0(x):
            return rest * target[x] + around(v0, x, *level0)

        for k in range(1, X1 - 1):
            t1[k] = coarse_row(residual0(2 * k), residual0(2 * k + 1), X1 + k)
        for k in range(1, X1 - 1):
            st = safe_step(d1[k], face1[k] + c1[k])
            step1[k] = st
            v1[k] = st * t1[k]

        def residual1(k):
            return rest * t1[k, :, 0:128] + around(v1, k, *level1)[:, 0:128]

        t2_own = message(residual1, 0)
        c2_own = message(lambda k: c1[k, :, 0:128], 1)
        lane_m = iota((mrows, 128), 1)
        own, got = (own0, got0) if n == 0 else (own1, got1)
        own[0:mrows] = jnp.where(lane_m < 64, t2_own, c2_own)
        if n == 0:
            own[mrows : 2 * mrows] = message(lambda k: d1[k, :, 0:128], 2)
        gather_send(n, own, got)
        v_copies = [
            (remote(v1.at[X1 - H1 - 2], hv1.at[n, 0], v_send.at[n, 0], v_recv.at[n, 0], right), has_right, has_left),
            (remote(v1.at[H1 + 1], hv1.at[n, 1], v_send.at[n, 1], v_recv.at[n, 1], left), has_left, has_right),
        ]
        for copy, can, _ in v_copies:
            pl.when(can)(copy.start)
        got[0, b] = own[...]
        gather_wait(n, got)
        lane2 = iota((rows2, 128), 1)
        mine2, low2, high2 = [got[i, :, 0:mrows, :].reshape(rows2, 128) for i in range(3)]
        t2 = jnp.where(lane2 < 64, mine2, pltpu.roll(jnp.where(lane2 < 32, high2, low2), 64, 1))
        c2 = jnp.where(lane2 < 64, pltpu.roll(mine2, 64, 1), jnp.where(lane2 < 96, high2, low2))
        if n == 0:
            mine2, low2, high2 = [got[i, :, mrows : 2 * mrows, :].reshape(rows2, 128) for i in range(3)]
            d2 = jnp.where(lane2 < 64, mine2, jnp.where(lane2 < 96, high2, low2))
            d3 = flat_coarse(d2, z2, 2)
            face2 = flat_weights(w2, d2, z2, 0.25**2)
            face3 = flat_weights(w3, d3, z3, 0.25**3)
        step2 = safe_step(d2, face2 + c2)
        v2 = step2 * t2
        t3 = flat_coarse(rest * t2 + flat_around(w2, v2, z2), z2, 0)
        c3 = flat_coarse(c2, z2, 1)
        step3 = safe_step(d3, face3 + c3)
        v3 = step3 * t3
        base = v3
        for repeat in range(COARSE - 1):
            v3 = (rest * v3 + base) + step3 * flat_around(w3, v3, z3)
        v2 = v2 + flat_fine(v3, z2)
        v2 = (rest * v2 + step2 * t2) + step2 * flat_around(w2, v2, z2)
        v2_ref[0:z2] = jnp.zeros((z2, 128), f32)
        v2_ref[z2 : z2 + rows2] = v2
        v2_ref[z2 + rows2 :] = jnp.zeros((z2, 128), f32)
        near = v2_ref[pl.ds(pl.multiple_of(b * mrows, 8), 2 * mrows), :]
        for i, index in enumerate((half, half_up)):
            wide = lanes_at(near, index)
            e_ref[i, pl.ds(0, 2 * mrows, stride=2), :] = wide
            e_ref[i, pl.ds(1, 2 * mrows, stride=2), :] = wide
        for copy, _, can in v_copies:
            pl.when(can)(copy.wait_recv)
        for k in range(X1):
            before = hv1[n, 0] if k == 0 else hv1[n, 1] if k == X1 - 1 else v1[k]
            at = (k // 2) * z1
            tmp2[k] = before + jnp.concatenate([e_ref[i, at : at + z1, :] for i in range(2)], axis=1)
        for k in range(1, X1 - 1):
            better = rest * tmp2[k] + step1[k] * (t1[k] + around(tmp2, k, *level1))
            fine = fine_row(better, k)
            for x in (2 * k, 2 * k + 1):
                v0[x] = v0[x] + fine
        out = range(H, H + cx) if n == 0 else range(H - 1, H + cx + 1)
        for x in out:
            new = rest * v0[x] + step0[x] * (target[x] + around(v0, x, *level0))
            if n == 0:
                pot[x] = new
            else:
                pot2[x] = pot[x] + new
        if n == 0:
            pot_copies = rows_both_ways(pot, pot, 5, slice(0, W0))
            for copy, can, _ in pot_copies:
                go(copy, can)
        for copy, can, _ in v_copies:
            pl.when(can)(copy.wait_send)

    zrow = iota((z0, y), 0)
    end = (zrow == 0) | (zrow == z0 - 1)
    for x in range(H, H + cx):
        here = pot2[x]
        mid = here[:, 0:y]
        for i in range(2):
            turned[0, i, pl.ds(x - H, nz, stride=cx), :] = mid[:, i * 128 : (i + 1) * 128]
        sh, _ = sinh_cosh(mid)
        total = wx[x, :, 0:y] * (mid - pot2[x + 1, :, 0:y]) + wx[x - 1, :, 0:y] * (mid - pot2[x - 1, :, 0:y])
        total = total + wzp[x, :, 0:y] * (mid - pltpu.roll(mid, z0 - 1, 0)) + wzm[x, :, 0:y] * (mid - pltpu.roll(mid, 1, 0))
        total = total + wyp[x, :, 0:y] * (mid - pltpu.roll(here, W0 - 1, 1)[:, 0:y])
        total = total + wym[x, :, 0:y] * (mid - pltpu.roll(here, 1, 1)[:, 0:y])
        total = total + jnp.where(end, 0.5 * d0[x, :, 0:y], 0.0) * mid
        total = total + rb[x, :, 0:y] * sh - src[x, :, 0:y]
        for i in range(2):
            turned[1, i, pl.ds(x - H, nz, stride=cx), :] = total[:, i * 128 : (i + 1) * 128]
    for i in range(2):
        pot_out[:, i * 128 : (i + 1) * 128] = turned[0, i]
        mis_out[:, i * 128 : (i + 1) * 128] = turned[1, i]

    for out, _ in slab_copies:
        out.wait_send()
    for copy, can in sent:
        pl.when(can)(copy.wait_send)
    gather_drain(0, got0)
    gather_drain(1, got1)


def per_device(atom_counts, ion_flags, charge_cells, charge_values):
    slabs, bulks = lax.axis_size("slab"), lax.axis_size("bulk")
    nz, cx, y = ion_flags.shape
    z1, z2, z3 = nz // 2, nz // 4, nz // 8
    X0, X1 = cx + 2 * H, cx // 2 + H
    W0, W1 = y + 128, y // 2 + 128
    arows = nz * cx // slabs
    mrows = 2 * z2
    rows2, rows3 = bulks * mrows, bulks * z3
    i32 = jnp.int32
    vm = pltpu.VMEM
    dma = pltpu.SemaphoreType.DMA

    def level0(n=X0):
        return vm((n, nz, W0), f32)

    def level1(n=X1):
        return vm((n, z1, W1), f32)

    pot, mis = pl.pallas_call(
        lambda *refs: solver(slabs, bulks, nz, cx, y, *refs),
        out_shape=[jax.ShapeDtypeStruct((nz * cx, y), f32)] * 2,
        in_specs=[pl.BlockSpec(memory_space=pl.ANY)] * 4,
        out_specs=[pl.BlockSpec(memory_space=pltpu.VMEM)] * 2,
        scratch_shapes=[
            vm(atom_counts.shape, i32), vm((2, nz * cx, 128), i32),
            vm((1,) + charge_cells.shape, i32), vm((1,) + charge_values.shape, f32),
            vm((slabs, arows, W0), f32), vm((slabs, arows, W0), f32),
            level0(3 * cx), level0(), level0(), vm((2, cx, nz, 128), f32), vm((2, cx, nz, 128), f32),
            level0(), level0(), level0(), level0(), level0(), level0(), level0(), level0(), level0(), level0(),
            level0(), level0(), level0(), level0(), vm((2 * X1, 3, nz, 128), f32),
            level1(), level1(), level1(), level1(), level1(), level1(), level1(), level1(), level1(), level1(),
            level1(), vm((2, 2, z1, W1), f32), vm((3, 2 * z1, 128), f32), level1(),
            vm((2 * mrows, 128), f32), vm((mrows, 128), f32),
            vm((3, bulks, 2 * mrows, 128), f32), vm((3, bulks, mrows, 128), f32),
            vm((6, rows2, 128), f32), vm((6, rows3, 128), f32),
            vm((rows2 + 2 * z2, 128), f32), vm((2, 4 * mrows, 128), f32), vm((3, rows2, 128), f32),
            vm((2, 2, nz * cx, 128), f32),
            dma((5,)), dma((slabs,)), dma((slabs,)), dma((6, 2)), dma((6, 2)), dma((2, 2)), dma((2, 2)),
            dma((2, 2)), dma((2, 2)), dma((2, 3)), dma((2, 3)),
        ],
        compiler_params=pltpu.CompilerParams(
            collective_id=0, has_side_effects=True, vmem_limit_bytes=60 << 20
        ),
    )(atom_counts, ion_flags.reshape(nz * cx, y), charge_cells[None], charge_values[None])
    return pot.reshape(nz, cx, y), mis.reshape(nz, cx, y)


def solution(mesh):
    placed = (
        P("slab", "bulk", None),
        P(None, "bulk", "slab"),
        P(("slab", "bulk")),
        P(("slab", "bulk")),
    )
    return jax.shard_map(
        per_device,
        mesh=mesh,
        in_specs=placed,
        out_specs=(P(None, "bulk", "slab"), P(None, "bulk", "slab")),
        check_vma=False,
    )
```

```python
import jax
import jax.numpy as jnp
import numpy as np
from jax import lax
from jax.experimental import pallas as pl
from jax.experimental.pallas import tpu as pltpu
from jax.sharding import PartitionSpec as P

COARSE = 8
NEWTON = 2
H = 4

taper_raw = np.exp(-0.5 * (np.arange(-4, 5) / 1.5) ** 2)
taper_weights = taper_raw / taper_raw.sum()
damping = 0.8
rest = 1.0 - damping
screening = 1.0
density_scale = 2.0

MESH_ID = pl.DeviceIdType.MESH
LN2 = float(np.log(2.0))
f32 = jnp.float32


def iota(shape, dim):
    return lax.broadcasted_iota(jnp.int32, shape, dim)


def log2(n):
    return int(n).bit_length() - 1


def mm(a, b):
    return lax.dot_general(
        a, b, (((1,), (0,)), ((), ())),
        precision=lax.Precision.HIGHEST, preferred_element_type=f32,
    )


def sinh_cosh(p):
    a, b = jnp.exp(p - LN2), jnp.exp(-p - LN2)
    q = jnp.minimum(p * p, 1.0)
    small = p * (
        1.0
        + q * (1 / 6) * (1.0 + q * (1 / 20) * (1.0 + q * (1 / 42) * (1.0 + q * (1 / 72) * (1.0 + q * (1 / 110)))))
    )
    return jnp.where(jnp.abs(p) < 1.0, small, a - b), a + b


def taper_y(density):
    width = density.shape[1]
    lane = iota(density.shape, 1)
    summed = float(taper_weights[4]) * density
    for k in range(1, 5):
        before = jnp.where(lane < k, 0.0, pltpu.roll(density, k, 1))
        after = jnp.where(lane >= width - k, 0.0, pltpu.roll(density, width - k, 1))
        summed = summed + float(taper_weights[4 + k]) * (before + after)
    return summed


def taper_z(rows, z, cx):
    i, j = iota((rows, rows), 0), iota((rows, rows), 1)
    far = jnp.abs((i & (z - 1)) - (j >> log2(cx)))
    band = jnp.zeros((rows, rows), f32)
    for k in range(5):
        band = jnp.where(far == k, float(taper_weights[4 + k]), band)
    return jnp.where((i >> log2(z)) == (j & (cx - 1)), band, 0.0)


def scattered(cells, values, rows, z, cx, y):
    entries = cells.shape[1]
    ly, lx = log2(y), log2(cx)
    row = ((cells >> ly) & (cx - 1)) * z + (cells >> (ly + lx))
    at_row = jnp.where(iota((rows, entries), 0) == row, values, 0.0)
    at_y = jnp.where(iota((y, entries), 0) == (cells & (y - 1)), f32(1.0), f32(0.0))
    return lax.dot_general(
        at_row, at_y, (((1,), (1,)), ((), ())),
        precision=lax.Precision.HIGHEST, preferred_element_type=f32,
    )


def lanes_at(v, index):
    parts = [
        jnp.take_along_axis(v[i : i + 8], index, axis=1, mode="promise_in_bounds")
        for i in range(0, v.shape[0], 8)
    ]
    return parts[0] if len(parts) == 1 else jnp.concatenate(parts, axis=0)


def halved(v, index):
    return lanes_at(v + pltpu.roll(v, 127, 1), index)


def solver(
    slabs, bulks, nz, cx, y,
    atoms_hbm, flags_hbm, cells_hbm, values_hbm, pot_out, mis_out,
    atoms_in, flags_in, cells_in, values_in,
    ay, abuf, nbuf, dens, opened, src, yout, yin, ycorner,
    d0, rb, wx, wyp, wym, wzp, wzm, face, c0, step0, v0, tgt, pot, pot2, tmp,
    d1, w1x, w1yp, w1ym, w1zp, w1zm, face1, c1, step1, t1, v1, hv1, tmp1, tmp2,
    own0, own1, side0, side1, got0, got1, gots0, gots1, w2, w3, v2_ref, e_ref, tmp3, turned,
    load_sem, a_send, a_recv, f_send, f_recv, x_send, x_recv, y_send, y_recv,
    v_send, v_recv, g_send, g_recv,
):
    s, b = lax.axis_index("slab"), lax.axis_index("bulk")
    z0, z1, z2, z3 = nz, nz // 2, nz // 4, nz // 8
    X0, X1 = cx + 2 * H, cx // 2 + H
    H1 = H // 2
    W0, W1 = y + 128, y // 2 + 128
    mrows = 2 * z2
    rows2, rows3 = bulks * mrows, bulks * z3
    at_left, at_right = b == 0, b == bulks - 1
    at_low, at_high = s == 0, s == slabs - 1
    has_left, has_right = b > 0, b < bulks - 1
    has_low, has_high = s > 0, s < slabs - 1

    loads = [
        pltpu.make_async_copy(there, here, load_sem.at[i])
        for i, (there, here) in enumerate((
            (atoms_hbm, atoms_in), (cells_hbm, cells_in), (values_hbm, values_in),
            (flags_hbm.at[:, 0:128], flags_in.at[0]), (flags_hbm.at[:, 128:256], flags_in.at[1]),
        ))
    ]
    for load in loads:
        load.start()

    def flip(at, k):
        for i in range(log2(k) + 1):
            if k >> i & 1:
                at = at + (1 << i) * (1 - 2 * (at // (1 << i) % 2))
        return at

    barrier = pltpu.get_barrier_semaphore()
    for k in range(1, slabs):
        pl.semaphore_signal(barrier, inc=1, device_id=(flip(s, k), b), device_id_type=MESH_ID)
    for k in range(1, bulks):
        pl.semaphore_signal(barrier, inc=1, device_id=(s, flip(b, k)), device_id_type=MESH_ID)

    def clear(*refs):
        for ref in refs:
            ref[...] = jnp.zeros(ref.shape, ref.dtype)

    @pl.when(at_left)
    def _():
        clear(nbuf.at[0], opened.at[0:H], src.at[0:H], ycorner.at[0], pot.at[0:H], hv1.at[0, 0], hv1.at[1, 0])

    @pl.when(at_right)
    def _():
        clear(
            nbuf.at[1], opened.at[H + cx : X0], src.at[H + cx : X0], ycorner.at[1],
            pot.at[H + cx : X0], hv1.at[0, 1], hv1.at[1, 1],
        )

    @pl.when(at_low)
    def _():
        clear(gots0.at[0], gots1.at[0], yin.at[0])

    @pl.when(at_high)
    def _():
        clear(gots0.at[1], gots1.at[1], yin.at[1])

    def remote(source, target, send, recv, to):
        return pltpu.make_async_remote_copy(
            src_ref=source, dst_ref=target, send_sem=send, recv_sem=recv,
            device_id=to, device_id_type=MESH_ID,
        )

    right, left = (s, b + 1), (s, b - 1)
    high, low = (s + 1, b), (s - 1, b)
    sent = []

    def go(copy, can):
        pl.when(can)(copy.start)
        sent.append((copy, can))

    loads[0].wait()
    smooth_y = taper_y(atoms_in[...].astype(f32).reshape(-1, slabs * y))
    arows = smooth_y.shape[0]
    planes = arows // cx
    lane_a = iota((arows, 128), 1)
    lane_c = iota((cx, 128), 1)
    nothing = jnp.zeros((arows, 128), f32)
    for t in range(slabs):
        for i in range(2):
            ay[t, i * arows : (i + 1) * arows] = smooth_y[:, t * y + i * 128 : t * y + (i + 1) * 128]
        after = smooth_y[:, (t + 1) * y : (t + 1) * y + 128] if t < slabs - 1 else nothing
        before = smooth_y[:, t * y - 128 : t * y] if t else nothing
        beside = jnp.where(lane_a < 64, after, before)
        packed = beside[0:cx]
        for g in range(1, planes):
            moved = pltpu.roll(beside[g * cx : (g + 1) * cx], 32 * g, 1)
            packed = jnp.where((((lane_c + 16) >> 5) & 3) == g, moved, packed)
        ay[t, 2 * arows :] = packed

    slab_copies = [
        (remote(ay.at[flip(s, k)], abuf.at[s], a_send.at[k], a_recv.at[k], (flip(s, k), b)),
         remote(ay.at[flip(s, k)], abuf.at[flip(s, k)], a_send.at[k], a_recv.at[k], (flip(s, k), b)))
        for k in range(1, slabs)
    ]
    pl.semaphore_wait(barrier, slabs + bulks - 2)
    for out, _ in slab_copies:
        out.start()

    def pass_on(k):
        which = flip(s, k) if k else s
        return [
            (remote(abuf.at[which], nbuf.at[0, which], f_send.at[k, 0], f_recv.at[k, 0], right), has_right, has_left),
            (remote(abuf.at[which], nbuf.at[1, which], f_send.at[k, 1], f_recv.at[k, 1], left), has_left, has_right),
        ]

    passed = []
    abuf[s] = ay[s]
    passed += pass_on(0)
    for copy, can, _ in passed:
        go(copy, can)

    for load in loads[1:]:
        load.wait()
    for x in range(cx):
        for i in range(2):
            flags = flags_in[i, pl.ds(x, nz, stride=cx), :]
            opened[H + x, :, i * 128 : (i + 1) * 128] = 1.0 - flags.astype(f32)
    charges = scattered(cells_in[...], values_in[...], cx * z0, z0, cx, y)
    for x in range(cx):
        src[H + x, :, 0:y] = charges[x * z0 : (x + 1) * z0]

    def rows_both_ways(source, target, slot, lanes):
        return [
            (remote(
                source.at[cx : cx + H, :, lanes], target.at[0:H, :, lanes],
                x_send.at[slot, 0], x_recv.at[slot, 0], right,
            ), has_right, has_left),
            (remote(
                source.at[H : 2 * H, :, lanes], target.at[H + cx : X0, :, lanes],
                x_send.at[slot, 1], x_recv.at[slot, 1], left,
            ), has_left, has_right),
        ]

    lane_h = iota((z0, 128), 1)
    for q in range(2):
        to_high = to_low = jnp.zeros((z0, 128), f32)
        for j in range(8):
            field = (opened, src)[j // 4]
            x = H + 4 * q + j % 4
            to_high = jnp.where(lane_h >> 4 == j, pltpu.roll(field[x, :, y - 128 : y], (16 * j + 16) % 128, 1), to_high)
            to_low = jnp.where(lane_h >> 4 == (j + 1) % 8, pltpu.roll(field[x, :, 0:128], (16 * j + 16) % 128, 1), to_low)
        yout[0, q], yout[1, q] = to_high, to_low
    y_copies = [
        (remote(yout.at[0], yin.at[0], y_send.at[0], y_recv.at[0], high), has_high, has_low),
        (remote(yout.at[1], yin.at[1], y_send.at[1], y_recv.at[1], low), has_low, has_high),
    ]
    x_copies = rows_both_ways(opened, opened, 0, slice(0, y)) + rows_both_ways(src, src, 1, slice(0, y))
    for copy, can, _ in y_copies + x_copies:
        go(copy, can)
    corner_copies = [
        (remote(yin.at[:, 1], ycorner.at[0], x_send.at[2, 0], x_recv.at[2, 0], right), has_right, has_left),
        (remote(yin.at[:, 0], ycorner.at[1], x_send.at[2, 1], x_recv.at[2, 1], left), has_left, has_right),
    ]

    along_z = taper_z(cx * z0, z0, cx)
    for k in range(1, slabs):
        slab_copies[k - 1][1].wait_recv()
        copies = pass_on(k)
        for copy, can, _ in copies:
            go(copy, can)
        passed += copies

    def smooth_z(pieces, at):
        columns = [pieces[:, i * arows : (i + 1) * arows].reshape(cx * z0, 128) for i in range(2)]
        edges = []
        for t in range(slabs):
            packed = pieces[t, 2 * arows :]
            edges += [packed] + [pltpu.roll(packed, 128 - 32 * g, 1) for g in range(1, planes)]
        columns.append(jnp.concatenate(edges, axis=0))
        for i, column in enumerate(columns):
            dens[at : at + cx, :, i * 128 : (i + 1) * 128] = mm(along_z, column).reshape(cx, z0, 128)

    for copy, _, can in y_copies:
        pl.when(can)(copy.wait_recv)
    for copy, can, _ in corner_copies:
        go(copy, can)
    smooth_z(abuf, cx)

    def unpack(x, from_low, from_high):
        for a, field in enumerate((opened, src)):
            j = 4 * a + x % 4
            both = jnp.where(lane_h >> 4 == j, from_low, from_high)
            both = pltpu.roll(both, (112 - 16 * j) % 128, 1)
            field[x, :, y:W0] = jnp.where((lane_h < 16) | (lane_h >= 112), both, 0.0)

    for x in range(H, H + cx):
        unpack(x, yin[0, x // 4 - 1], yin[1, x // 4 - 1])
    lane0 = iota((z0, W0), 1)
    keep_low = jnp.where(at_low, f32(0.0), f32(1.0))
    keep_high = jnp.where(at_high, f32(0.0), f32(1.0))
    keep_y = jnp.where(lane0 < y, 1.0, jnp.where(lane0 < y + 64, keep_high, keep_low))
    keep_left = jnp.where(at_left, f32(0.0), f32(1.0))
    keep_right = jnp.where(at_right, f32(0.0), f32(1.0))
    zrow0 = iota((z0, W0), 0)
    lane128 = iota((8, 128), 1)
    even = (2 * lane128) & 127
    half = lane128 >> 1
    half_up = 64 + half
    half_split = jnp.where(lane128 < 64, half, half_up)

    for copy, _, can in x_copies + corner_copies:
        pl.when(can)(copy.wait_recv)
    for x in range(H):
        unpack(x, ycorner[0, 0], ycorner[0, 1])
        unpack(H + cx + x, ycorner[1, 0], ycorner[1, 1])
    for copy, _, can in passed:
        pl.when(can)(copy.wait_recv)
    smooth_z(nbuf.at[0], 0)
    smooth_z(nbuf.at[1], 2 * cx)
    for x in range(X0):
        smoothed = float(taper_weights[4]) * dens[x + 4]
        for k in range(1, 5):
            smoothed = smoothed + float(taper_weights[4 + k]) * (dens[x + 4 - k] + dens[x + 4 + k])
        shading = jnp.exp(-smoothed / density_scale)
        keep = keep_y
        if x < H:
            keep = keep_y * keep_left
        elif x >= H + cx:
            keep = keep_y * keep_right
        d0[x] = keep * (2.0 + 78.0 * shading)
        rb[x] = screening * shading * shading * opened[x]

    def weights(d, wx, wyp, wym, wzp, wzm, face, scale):
        n, z, w = d.shape
        zrow = iota((z, w), 0)
        for x in range(n):
            if x < n - 1:
                wx[x] = (0.5 * scale) * (d[x] + d[x + 1])
        for x in range(1, n - 1):
            v = d[x]
            yp = (0.5 * scale) * (v + pltpu.roll(v, w - 1, 1))
            ym = (0.5 * scale) * (v + pltpu.roll(v, 1, 1))
            zp = jnp.where(zrow == z - 1, 0.0, (0.5 * scale) * (v + pltpu.roll(v, z - 1, 0)))
            zm = jnp.where(zrow == 0, 0.0, (0.5 * scale) * (v + pltpu.roll(v, 1, 0)))
            wyp[x], wym[x], wzp[x], wzm[x] = yp, ym, zp, zm
            ends = jnp.where((zrow == 0) | (zrow == z - 1), (0.5 * scale) * v, 0.0)
            face[x] = wx[x - 1] + wx[x] + yp + ym + zp + zm + ends

    def around(v, x, wx, wyp, wym, wzp, wzm):
        here = v[x]
        z, w = here.shape
        return (
            (wx[x] * v[x + 1] + wx[x - 1] * v[x - 1])
            + (wzp[x] * pltpu.roll(here, z - 1, 0) + wzm[x] * pltpu.roll(here, 1, 0))
            + (wyp[x] * pltpu.roll(here, w - 1, 1) + wym[x] * pltpu.roll(here, 1, 1))
        )

    level0 = (wx, wyp, wym, wzp, wzm)
    level1 = (w1x, w1yp, w1ym, w1zp, w1zm)

    def coarse_row(a, c, slot):
        both = a + c
        lane = iota((z1, 128), 1)
        parts = []
        for i in range(3):
            tmp[slot, i] = both[:, i * 128 : (i + 1) * 128]
            parts.append(halved(
                tmp[slot, i, pl.ds(0, z1, stride=2), :] + tmp[slot, i, pl.ds(1, z1, stride=2), :], even
            ))
        return 0.125 * jnp.concatenate([jnp.where(lane < 64, parts[0], parts[1]), parts[2]], axis=1)

    def fine_row(c, slot):
        for i, index in enumerate((half, half_up, half_split)):
            wide = lanes_at(c[:, 128 * (i // 2) : 128 * (i // 2) + 128], index)
            tmp[slot, i, pl.ds(0, z1, stride=2), :] = wide
            tmp[slot, i, pl.ds(1, z1, stride=2), :] = wide
        return jnp.concatenate([tmp[slot, i] for i in range(3)], axis=1)

    def message(f, slot):
        for k in range(2):
            tmp1[slot, k * z1 : (k + 1) * z1, :] = f(H1 + 2 * k) + f(H1 + 2 * k + 1)
        w = tmp1[slot, pl.ds(0, mrows, stride=2), :] + tmp1[slot, pl.ds(1, mrows, stride=2), :]
        return 0.125 * halved(w, even)

    def safe_step(d, diagonal):
        return jnp.where(d > 0.0, damping / diagonal, 0.0)

    def gather_send(n, own, side, got, gots):
        for k in range(bulks - 1, 0, -1):
            remote(own, got.at[b], g_send.at[n, 2], g_recv.at[n, 2], (s, flip(b, k))).start()
        for i, (can, row) in enumerate(((has_high, s + 1), (has_low, s - 1))):
            @pl.when(can)
            def _():
                for k in range(bulks - 1, -1, -1):
                    remote(
                        side.at[i], gots.at[i, b], g_send.at[n, i], g_recv.at[n, i],
                        (row, flip(b, k) if k else b),
                    ).start()

    def gather_copy(n, got, gots, i):
        part = got.at[0 : bulks - 1] if i == 2 else gots.at[i]
        return remote(part, part, g_send.at[n, i], g_recv.at[n, i], (s, flip(b, 1)))

    def gather_wait(n, got, gots):
        gather_copy(n, got, gots, 2).wait_recv()
        pl.when(has_low)(gather_copy(n, got, gots, 0).wait_recv)
        pl.when(has_high)(gather_copy(n, got, gots, 1).wait_recv)

    def gather_drain(n, got, gots):
        gather_copy(n, got, gots, 2).wait_send()
        pl.when(has_high)(gather_copy(n, got, gots, 0).wait_send)
        pl.when(has_low)(gather_copy(n, got, gots, 1).wait_send)

    def flat_weights(w_ref, d, z, scale):
        rows = d.shape[0]
        row = iota(d.shape, 0)
        zrow = row & (z - 1)
        total = None
        for i, (outside, other) in enumerate((
            (row < z, pltpu.roll(d, z, 0)), (row >= rows - z, pltpu.roll(d, rows - z, 0)),
            (zrow == 0, pltpu.roll(d, 1, 0)), (zrow == z - 1, pltpu.roll(d, rows - 1, 0)),
            (None, pltpu.roll(d, 1, 1)), (None, pltpu.roll(d, 127, 1)),
        )):
            w = (0.5 * scale) * (d + other)
            if outside is None:
                w_ref[i] = w
            else:
                w_ref[i] = jnp.where(outside, 0.0, w)
                w = jnp.where(outside, (0.5 * scale) * d, w)
            total = w if total is None else total + w
        return total

    def flat_around(w_ref, v, z):
        rows = v.shape[0]
        return (
            (w_ref[4] * pltpu.roll(v, 1, 1) + w_ref[5] * pltpu.roll(v, 127, 1))
            + ((w_ref[0] * pltpu.roll(v, z, 0) + w_ref[1] * pltpu.roll(v, rows - z, 0))
               + (w_ref[2] * pltpu.roll(v, 1, 0) + w_ref[3] * pltpu.roll(v, rows - 1, 0)))
        )

    def flat_coarse(v, z, slot):
        rows = v.shape[0]
        tmp3[slot] = v
        w = tmp3[slot, pl.ds(0, rows // 2, stride=2), :] + tmp3[slot, pl.ds(1, rows // 2, stride=2), :]
        zc = z // 2
        pieces = [w[(2 * k) * zc : (2 * k + 1) * zc] + w[(2 * k + 1) * zc : (2 * k + 2) * zc] for k in range(rows // (4 * zc))]
        return 0.125 * halved(jnp.concatenate(pieces, axis=0), even)

    def flat_fine(v, z):
        wide = lanes_at(v, half)
        zc = z // 2
        pieces = []
        for k in range(v.shape[0] // zc):
            pieces += [wide[k * zc : (k + 1) * zc]] * 2
        doubled = jnp.concatenate(pieces, axis=0)
        rows = 4 * v.shape[0]
        tmp3[0, pl.ds(0, rows // 2, stride=2), :] = doubled
        tmp3[0, pl.ds(1, rows // 2, stride=2), :] = doubled
        return tmp3[0]

    weights(d0, *level0, face, 1.0)
    for k in range(X1):
        d1[k] = coarse_row(d0[2 * k], d0[2 * k + 1], k)
    weights(d1, *level1, face1, 0.25)
    face2 = face3 = None
    d2 = None

    for n in range(NEWTON):
        inner = range(1, X0 - 1)
        if n == 0:
            target, c_of = src, rb
        else:
            target, c_of = tgt, c0

            def reaction(x):
                sh, ch = sinh_cosh(pot[x])
                c0[x] = rb[x] * ch
                if x in inner:
                    tgt[x] = src[x] - rb[x] * sh
                    return True

            def misfit_row(x):
                tgt[x] = tgt[x] - face[x] * pot[x] + around(pot, x, *level0)

            mine = range(H, H + cx)
            for x in mine:
                reaction(x)
            for x in mine[1:-1]:
                misfit_row(x)
            for copy, _, can in pot_copies:
                pl.when(can)(copy.wait_recv)
            for x in range(X0):
                if x not in mine:
                    reaction(x)
            for x in inner:
                if x not in mine[1:-1]:
                    misfit_row(x)
        for x in inner:
            st = safe_step(d0[x], face[x] + c_of[x])
            step0[x] = st
            v0[x] = st * target[x]
        for k in range(X1):
            c1[k] = coarse_row(c_of[2 * k], c_of[2 * k + 1], k)

        def residual0(x):
            return rest * target[x] + around(v0, x, *level0)

        for k in range(1, X1 - 1):
            t1[k] = coarse_row(residual0(2 * k), residual0(2 * k + 1), X1 + k)
        for k in range(1, X1 - 1):
            st = safe_step(d1[k], face1[k] + c1[k])
            step1[k] = st
            v1[k] = st * t1[k]

        def residual1(k):
            return rest * t1[k, :, 0:128] + around(v1, k, *level1)[:, 0:128]

        t2_own = message(residual1, 0)
        c2_own = message(lambda k: c1[k, :, 0:128], 1)
        lane_m = iota((mrows, 128), 1)
        own, side, got, gots = (own0, side0, got0, gots0) if n == 0 else (own1, side1, got1, gots1)
        own[0:mrows] = jnp.where(lane_m < 64, t2_own, c2_own)
        to_high = jnp.where(lane_m < 64, c2_own, t2_own)
        to_low = to_high
        if n == 0:
            d2_own = message(lambda k: d1[k, :, 0:128], 2)
            own[mrows : 2 * mrows] = d2_own
            moved = pltpu.roll(d2_own, 32, 1)
            to_high = jnp.where(lane_m >> 5 == 2, moved, to_high)
            to_low = jnp.where(lane_m >> 5 == 3, moved, to_low)
        side[0], side[1] = to_high, to_low
        gather_send(n, own, side, got, gots)
        v_copies = [
            (remote(v1.at[X1 - H1 - 2], hv1.at[n, 0], v_send.at[n, 0], v_recv.at[n, 0], right), has_right, has_left),
            (remote(v1.at[H1 + 1], hv1.at[n, 1], v_send.at[n, 1], v_recv.at[n, 1], left), has_left, has_right),
        ]
        for copy, can, _ in v_copies:
            pl.when(can)(copy.start)
        got[b] = own[...]
        gather_wait(n, got, gots)
        lane2 = iota((rows2, 128), 1)
        mine2, low2, high2 = [ref.reshape(rows2, 128) for ref in (got[:, 0:mrows], gots[0], gots[1])]
        t2 = jnp.where(lane2 < 64, mine2, jnp.where(lane2 < 96, high2, low2))
        c2 = pltpu.roll(jnp.where(lane2 >= 64, mine2, jnp.where(lane2 < 32, high2, low2)), 64, 1)
        if n == 0:
            d2 = jnp.where(
                lane2 < 64, got[:, mrows : 2 * mrows].reshape(rows2, 128),
                jnp.where(lane2 < 96, pltpu.roll(high2, 96, 1), pltpu.roll(low2, 32, 1)),
            )
            d3 = flat_coarse(d2, z2, 2)
            face2 = flat_weights(w2, d2, z2, 0.25**2)
            face3 = flat_weights(w3, d3, z3, 0.25**3)
        step2 = safe_step(d2, face2 + c2)
        v2 = step2 * t2
        t3 = flat_coarse(rest * t2 + flat_around(w2, v2, z2), z2, 0)
        c3 = flat_coarse(c2, z2, 1)
        step3 = safe_step(d3, face3 + c3)
        v3 = step3 * t3
        base = v3
        for repeat in range(COARSE - 1):
            v3 = (rest * v3 + base) + step3 * flat_around(w3, v3, z3)
        v2 = v2 + flat_fine(v3, z2)
        v2 = (rest * v2 + step2 * t2) + step2 * flat_around(w2, v2, z2)
        v2_ref[0:z2] = jnp.zeros((z2, 128), f32)
        v2_ref[z2 : z2 + rows2] = v2
        v2_ref[z2 + rows2 :] = jnp.zeros((z2, 128), f32)
        near = v2_ref[pl.ds(pl.multiple_of(b * mrows, 8), 2 * mrows), :]
        for i, index in enumerate((half, half_up)):
            wide = lanes_at(near, index)
            e_ref[i, pl.ds(0, 2 * mrows, stride=2), :] = wide
            e_ref[i, pl.ds(1, 2 * mrows, stride=2), :] = wide
        for copy, _, can in v_copies:
            pl.when(can)(copy.wait_recv)
        for k in range(X1):
            before = hv1[n, 0] if k == 0 else hv1[n, 1] if k == X1 - 1 else v1[k]
            at = (k // 2) * z1
            tmp2[k] = before + jnp.concatenate([e_ref[i, at : at + z1, :] for i in range(2)], axis=1)
        for k in range(1, X1 - 1):
            better = rest * tmp2[k] + step1[k] * (t1[k] + around(tmp2, k, *level1))
            fine = fine_row(better, k)
            for x in (2 * k, 2 * k + 1):
                v0[x] = v0[x] + fine
        out = range(H, H + cx) if n == 0 else range(H - 1, H + cx + 1)
        for x in out:
            new = rest * v0[x] + step0[x] * (target[x] + around(v0, x, *level0))
            if n == 0:
                pot[x] = new
            else:
                pot2[x] = pot[x] + new
        if n == 0:
            pot_copies = rows_both_ways(pot, pot, 3, slice(0, W0))
            for copy, can, _ in pot_copies:
                go(copy, can)
        for copy, can, _ in v_copies:
            pl.when(can)(copy.wait_send)

    zrow = iota((z0, y), 0)
    end = (zrow == 0) | (zrow == z0 - 1)
    for x in range(H, H + cx):
        here = pot2[x]
        mid = here[:, 0:y]
        for i in range(2):
            turned[0, i, pl.ds(x - H, nz, stride=cx), :] = mid[:, i * 128 : (i + 1) * 128]
        sh, _ = sinh_cosh(mid)
        total = wx[x, :, 0:y] * (mid - pot2[x + 1, :, 0:y]) + wx[x - 1, :, 0:y] * (mid - pot2[x - 1, :, 0:y])
        total = total + wzp[x, :, 0:y] * (mid - pltpu.roll(mid, z0 - 1, 0)) + wzm[x, :, 0:y] * (mid - pltpu.roll(mid, 1, 0))
        total = total + wyp[x, :, 0:y] * (mid - pltpu.roll(here, W0 - 1, 1)[:, 0:y])
        total = total + wym[x, :, 0:y] * (mid - pltpu.roll(here, 1, 1)[:, 0:y])
        total = total + jnp.where(end, 0.5 * d0[x, :, 0:y], 0.0) * mid
        total = total + rb[x, :, 0:y] * sh - src[x, :, 0:y]
        for i in range(2):
            turned[1, i, pl.ds(x - H, nz, stride=cx), :] = total[:, i * 128 : (i + 1) * 128]
    for i in range(2):
        pot_out[:, i * 128 : (i + 1) * 128] = turned[0, i]
        mis_out[:, i * 128 : (i + 1) * 128] = turned[1, i]

    for out, _ in slab_copies:
        out.wait_send()
    for copy, can in sent:
        pl.when(can)(copy.wait_send)
    gather_drain(0, got0, gots0)
    gather_drain(1, got1, gots1)


def per_device(atom_counts, ion_flags, charge_cells, charge_values):
    slabs, bulks = lax.axis_size("slab"), lax.axis_size("bulk")
    nz, cx, y = ion_flags.shape
    z1, z2, z3 = nz // 2, nz // 4, nz // 8
    X0, X1 = cx + 2 * H, cx // 2 + H
    W0, W1 = y + 128, y // 2 + 128
    arows = nz * cx // slabs
    piece = 2 * arows + cx
    mrows = 2 * z2
    rows2, rows3 = bulks * mrows, bulks * z3
    i32 = jnp.int32
    vm = pltpu.VMEM
    dma = pltpu.SemaphoreType.DMA

    def level0(n=X0):
        return vm((n, nz, W0), f32)

    def level1(n=X1):
        return vm((n, z1, W1), f32)

    pot, mis = pl.pallas_call(
        lambda *refs: solver(slabs, bulks, nz, cx, y, *refs),
        out_shape=[jax.ShapeDtypeStruct((nz * cx, y), f32)] * 2,
        in_specs=[pl.BlockSpec(memory_space=pl.ANY)] * 4,
        out_specs=[pl.BlockSpec(memory_space=pltpu.VMEM)] * 2,
        scratch_shapes=[
            vm(atom_counts.shape, i32), vm((2, nz * cx, 128), i32),
            vm((1,) + charge_cells.shape, i32), vm((1,) + charge_values.shape, f32),
            vm((slabs, piece, 128), f32), vm((slabs, piece, 128), f32), vm((2, slabs, piece, 128), f32),
            level0(3 * cx), level0(), level0(),
            vm((2, 2, nz, 128), f32), vm((2, 2, nz, 128), f32), vm((2, 2, nz, 128), f32),
            level0(), level0(), level0(), level0(), level0(), level0(), level0(), level0(), level0(), level0(),
            level0(), level0(), level0(), level0(), vm((2 * X1, 3, nz, 128), f32),
            level1(), level1(), level1(), level1(), level1(), level1(), level1(), level1(), level1(), level1(),
            level1(), vm((2, 2, z1, W1), f32), vm((3, 2 * z1, 128), f32), level1(),
            vm((2 * mrows, 128), f32), vm((mrows, 128), f32), vm((2, mrows, 128), f32), vm((2, mrows, 128), f32),
            vm((bulks, 2 * mrows, 128), f32), vm((bulks, mrows, 128), f32),
            vm((2, bulks, mrows, 128), f32), vm((2, bulks, mrows, 128), f32),
            vm((6, rows2, 128), f32), vm((6, rows3, 128), f32),
            vm((rows2 + 2 * z2, 128), f32), vm((2, 4 * mrows, 128), f32), vm((3, rows2, 128), f32),
            vm((2, 2, nz * cx, 128), f32),
            dma((5,)), dma((slabs,)), dma((slabs,)), dma((slabs, 2)), dma((slabs, 2)),
            dma((4, 2)), dma((4, 2)), dma((2,)), dma((2,)),
            dma((2, 2)), dma((2, 2)), dma((2, 3)), dma((2, 3)),
        ],
        compiler_params=pltpu.CompilerParams(
            collective_id=0, has_side_effects=True, vmem_limit_bytes=60 << 20
        ),
    )(atom_counts, ion_flags.reshape(nz * cx, y), charge_cells[None], charge_values[None])
    return pot.reshape(nz, cx, y), mis.reshape(nz, cx, y)


def solution(mesh):
    placed = (
        P("slab", "bulk", None),
        P(None, "bulk", "slab"),
        P(("slab", "bulk")),
        P(("slab", "bulk")),
    )
    return jax.shard_map(
        per_device,
        mesh=mesh,
        in_specs=placed,
        out_specs=(P(None, "bulk", "slab"), P(None, "bulk", "slab")),
        check_vma=False,
    )
```

```python
import jax
import jax.numpy as jnp
import numpy as np
from jax import lax
from jax.experimental import pallas as pl
from jax.experimental.pallas import tpu as pltpu
from jax.sharding import PartitionSpec as P

COARSE = 8
NEWTON = 2
H = 4

taper_raw = np.exp(-0.5 * (np.arange(-4, 5) / 1.5) ** 2)
taper_weights = taper_raw / taper_raw.sum()
damping = 0.8
rest = 1.0 - damping
screening = 1.0
density_scale = 2.0

MESH_ID = pl.DeviceIdType.MESH
LN2 = float(np.log(2.0))
f32 = jnp.float32


def iota(shape, dim):
    return lax.broadcasted_iota(jnp.int32, shape, dim)


def log2(n):
    return int(n).bit_length() - 1


def mm(a, b):
    return lax.dot_general(
        a, b, (((1,), (0,)), ((), ())),
        precision=lax.Precision.HIGHEST, preferred_element_type=f32,
    )


def sinh_cosh(p):
    a, b = jnp.exp(p - LN2), jnp.exp(-p - LN2)
    q = jnp.minimum(p * p, 1.0)
    small = p * (
        1.0
        + q * (1 / 6) * (1.0 + q * (1 / 20) * (1.0 + q * (1 / 42) * (1.0 + q * (1 / 72) * (1.0 + q * (1 / 110)))))
    )
    return jnp.where(jnp.abs(p) < 1.0, small, a - b), a + b


def taper_y(density):
    width = density.shape[1]
    lane = iota(density.shape, 1)
    summed = float(taper_weights[4]) * density
    for k in range(1, 5):
        before = jnp.where(lane < k, 0.0, pltpu.roll(density, k, 1))
        after = jnp.where(lane >= width - k, 0.0, pltpu.roll(density, width - k, 1))
        summed = summed + float(taper_weights[4 + k]) * (before + after)
    return summed


def taper_z(rows, z, cx):
    i, j = iota((rows, rows), 0), iota((rows, rows), 1)
    far = jnp.abs((i & (z - 1)) - (j >> log2(cx)))
    band = jnp.zeros((rows, rows), f32)
    for k in range(5):
        band = jnp.where(far == k, float(taper_weights[4 + k]), band)
    return jnp.where((i >> log2(z)) == (j & (cx - 1)), band, 0.0)


def scattered(cells, values, rows, z, cx, y):
    entries = cells.shape[1]
    ly, lx = log2(y), log2(cx)
    row = ((cells >> ly) & (cx - 1)) * z + (cells >> (ly + lx))
    at_row = jnp.where(iota((rows, entries), 0) == row, values, 0.0)
    at_y = jnp.where(iota((y, entries), 0) == (cells & (y - 1)), f32(1.0), f32(0.0))
    return lax.dot_general(
        at_row, at_y, (((1,), (1,)), ((), ())),
        precision=lax.Precision.HIGHEST, preferred_element_type=f32,
    )


def lanes_at(v, index):
    parts = [
        jnp.take_along_axis(v[i : i + 8], index, axis=1, mode="promise_in_bounds")
        for i in range(0, v.shape[0], 8)
    ]
    return parts[0] if len(parts) == 1 else jnp.concatenate(parts, axis=0)


def halved(v, index):
    return lanes_at(v + pltpu.roll(v, 127, 1), index)


def solver(
    slabs, bulks, nz, cx, y,
    atoms_hbm, flags_hbm, cells_hbm, values_hbm, pot_out, mis_out,
    atoms_in, flags_in, cells_in, values_in,
    ay, abuf, nbuf, dens, opened, src, yout, yin, ycorner,
    d0, d_far, rb, wx, wyp, wym, wzp, wzm, face, c0, step0, v0, v_far, vb, tgt, pot, pot2, tmp,
    d1, w1x, w1yp, w1ym, w1zp, w1zm, face1, c1, step1, t1, v1, hv1, tmp1, tmp2,
    own0, own1, side0, side1, got0, got1, gots0, gots1, w2, w3, v2_ref, e_ref, tmp3, turned,
    load_sem, a_send, a_recv, f_send, f_recv, x_send, x_recv, y_send, y_recv,
    e_send, e_recv, g_send, g_recv,
):
    s, b = lax.axis_index("slab"), lax.axis_index("bulk")
    z0, z1, z2, z3 = nz, nz // 2, nz // 4, nz // 8
    X0, X1 = cx + 2 * H, cx // 2 + 2 * H
    W0, W1 = y + 128, y // 2 + 128
    mrows = 2 * z2
    rows2, rows3 = bulks * mrows, bulks * z3
    at_left, at_right = b == 0, b == bulks - 1
    at_low, at_high = s == 0, s == slabs - 1
    has_left, has_right = b > 0, b < bulks - 1
    has_low, has_high = s > 0, s < slabs - 1

    loads = [
        pltpu.make_async_copy(there, here, load_sem.at[i])
        for i, (there, here) in enumerate((
            (atoms_hbm, atoms_in), (cells_hbm, cells_in), (values_hbm, values_in),
            (flags_hbm.at[:, 0:128], flags_in.at[0]), (flags_hbm.at[:, 128:256], flags_in.at[1]),
        ))
    ]
    for load in loads:
        load.start()

    def flip(at, k):
        for i in range(log2(k) + 1):
            if k >> i & 1:
                at = at + (1 << i) * (1 - 2 * (at // (1 << i) % 2))
        return at

    barrier = pltpu.get_barrier_semaphore()
    for k in range(1, slabs):
        pl.semaphore_signal(barrier, inc=1, device_id=(flip(s, k), b), device_id_type=MESH_ID)
    for k in range(1, bulks):
        pl.semaphore_signal(barrier, inc=1, device_id=(s, flip(b, k)), device_id_type=MESH_ID)

    def clear(*refs):
        for ref in refs:
            ref[...] = jnp.zeros(ref.shape, ref.dtype)

    @pl.when(at_left)
    def _():
        clear(nbuf.at[0], opened.at[0:H], src.at[0:H], ycorner.at[0], hv1.at[0], d_far.at[0], v_far.at[0],
              d1.at[0:2], c1.at[1], t1.at[1:3], v1.at[0])

    @pl.when(at_right)
    def _():
        clear(
            nbuf.at[1], opened.at[H + cx : X0], src.at[H + cx : X0], ycorner.at[1],
            hv1.at[1], d_far.at[1], v_far.at[1], d1.at[X1 - 2 : X1], c1.at[X1 - 2], t1.at[X1 - 3 : X1 - 1], v1.at[X1 - 1],
        )

    @pl.when(at_low)
    def _():
        clear(gots0.at[0], gots1.at[0], yin.at[0])

    @pl.when(at_high)
    def _():
        clear(gots0.at[1], gots1.at[1], yin.at[1])

    def remote(source, target, send, recv, to):
        return pltpu.make_async_remote_copy(
            src_ref=source, dst_ref=target, send_sem=send, recv_sem=recv,
            device_id=to, device_id_type=MESH_ID,
        )

    right, left = (s, b + 1), (s, b - 1)
    high, low = (s + 1, b), (s - 1, b)
    sent = []

    def go(copy, can):
        pl.when(can)(copy.start)
        sent.append((copy, can))

    loads[0].wait()
    smooth_y = taper_y(atoms_in[...].astype(f32).reshape(-1, slabs * y))
    arows = smooth_y.shape[0]
    planes = arows // cx
    lane_a = iota((arows, 128), 1)
    lane_c = iota((cx, 128), 1)
    nothing = jnp.zeros((arows, 128), f32)
    for t in range(slabs):
        for i in range(2):
            ay[t, i * arows : (i + 1) * arows] = smooth_y[:, t * y + i * 128 : t * y + (i + 1) * 128]
        after = smooth_y[:, (t + 1) * y : (t + 1) * y + 128] if t < slabs - 1 else nothing
        before = smooth_y[:, t * y - 128 : t * y] if t else nothing
        beside = jnp.where(lane_a < 64, after, before)
        packed = beside[0:cx]
        for g in range(1, planes):
            moved = pltpu.roll(beside[g * cx : (g + 1) * cx], 32 * g, 1)
            packed = jnp.where((((lane_c + 16) >> 5) & 3) == g, moved, packed)
        ay[t, 2 * arows :] = packed

    slab_copies = [
        (remote(ay.at[flip(s, k)], abuf.at[s], a_send.at[k], a_recv.at[k], (flip(s, k), b)),
         remote(ay.at[flip(s, k)], abuf.at[flip(s, k)], a_send.at[k], a_recv.at[k], (flip(s, k), b)))
        for k in range(1, slabs)
    ]
    pl.semaphore_wait(barrier, slabs + bulks - 2)
    for out, _ in slab_copies:
        out.start()

    def pass_on(k):
        which = flip(s, k) if k else s
        return [
            (remote(abuf.at[which], nbuf.at[0, which], f_send.at[k, 0], f_recv.at[k, 0], right), has_right, has_left),
            (remote(abuf.at[which], nbuf.at[1, which], f_send.at[k, 1], f_recv.at[k, 1], left), has_left, has_right),
        ]

    passed = []
    abuf[s] = ay[s]
    passed += pass_on(0)
    for copy, can, _ in passed:
        go(copy, can)

    for load in loads[1:]:
        load.wait()
    for x in range(cx):
        for i in range(2):
            flags = flags_in[i, pl.ds(x, nz, stride=cx), :]
            opened[H + x, :, i * 128 : (i + 1) * 128] = 1.0 - flags.astype(f32)
    charges = scattered(cells_in[...], values_in[...], cx * z0, z0, cx, y)
    for x in range(cx):
        src[H + x, :, 0:y] = charges[x * z0 : (x + 1) * z0]

    def rows_both_ways(source, target, slot, lanes):
        return [
            (remote(
                source.at[cx : cx + H, :, lanes], target.at[0:H, :, lanes],
                x_send.at[slot, 0], x_recv.at[slot, 0], right,
            ), has_right, has_left),
            (remote(
                source.at[H : 2 * H, :, lanes], target.at[H + cx : X0, :, lanes],
                x_send.at[slot, 1], x_recv.at[slot, 1], left,
            ), has_left, has_right),
        ]

    lane_h = iota((z0, 128), 1)
    for q in range(2):
        to_high = to_low = jnp.zeros((z0, 128), f32)
        for j in range(8):
            field = (opened, src)[j // 4]
            x = H + 4 * q + j % 4
            to_high = jnp.where(lane_h >> 4 == j, pltpu.roll(field[x, :, y - 128 : y], (16 * j + 16) % 128, 1), to_high)
            to_low = jnp.where(lane_h >> 4 == (j + 1) % 8, pltpu.roll(field[x, :, 0:128], (16 * j + 16) % 128, 1), to_low)
        yout[0, q], yout[1, q] = to_high, to_low
    y_copies = [
        (remote(yout.at[0], yin.at[0], y_send.at[0], y_recv.at[0], high), has_high, has_low),
        (remote(yout.at[1], yin.at[1], y_send.at[1], y_recv.at[1], low), has_low, has_high),
    ]
    x_copies = rows_both_ways(opened, opened, 0, slice(0, y)) + rows_both_ways(src, src, 1, slice(0, y))
    for copy, can, _ in y_copies + x_copies:
        go(copy, can)
    corner_copies = [
        (remote(yin.at[:, 1], ycorner.at[0], x_send.at[2, 0], x_recv.at[2, 0], right), has_right, has_left),
        (remote(yin.at[:, 0], ycorner.at[1], x_send.at[2, 1], x_recv.at[2, 1], left), has_left, has_right),
    ]

    along_z = taper_z(cx * z0, z0, cx)
    for k in range(1, slabs):
        slab_copies[k - 1][1].wait_recv()
        copies = pass_on(k)
        for copy, can, _ in copies:
            go(copy, can)
        passed += copies

    def smooth_z(pieces, at):
        columns = [pieces[:, i * arows : (i + 1) * arows].reshape(cx * z0, 128) for i in range(2)]
        edges = []
        for t in range(slabs):
            packed = pieces[t, 2 * arows :]
            edges += [packed] + [pltpu.roll(packed, 128 - 32 * g, 1) for g in range(1, planes)]
        columns.append(jnp.concatenate(edges, axis=0))
        for i, column in enumerate(columns):
            dens[at : at + cx, :, i * 128 : (i + 1) * 128] = mm(along_z, column).reshape(cx, z0, 128)

    for copy, _, can in y_copies:
        pl.when(can)(copy.wait_recv)
    for copy, can, _ in corner_copies:
        go(copy, can)
    smooth_z(abuf, cx)

    def unpack(x, from_low, from_high):
        for a, field in enumerate((opened, src)):
            j = 4 * a + x % 4
            both = jnp.where(lane_h >> 4 == j, from_low, from_high)
            both = pltpu.roll(both, (112 - 16 * j) % 128, 1)
            field[x, :, y:W0] = jnp.where((lane_h < 16) | (lane_h >= 112), both, 0.0)

    for x in range(H, H + cx):
        unpack(x, yin[0, x // 4 - 1], yin[1, x // 4 - 1])
    lane0 = iota((z0, W0), 1)
    keep_low = jnp.where(at_low, f32(0.0), f32(1.0))
    keep_high = jnp.where(at_high, f32(0.0), f32(1.0))
    keep_y = jnp.where(lane0 < y, 1.0, jnp.where(lane0 < y + 64, keep_high, keep_low))
    keep_left = jnp.where(at_left, f32(0.0), f32(1.0))
    keep_right = jnp.where(at_right, f32(0.0), f32(1.0))
    zrow0 = iota((z0, W0), 0)
    lane128 = iota((8, 128), 1)
    even = (2 * lane128) & 127
    half = lane128 >> 1
    half_up = 64 + half
    half_split = jnp.where(lane128 < 64, half, half_up)

    for copy, _, can in x_copies + corner_copies:
        pl.when(can)(copy.wait_recv)
    for x in range(H):
        unpack(x, ycorner[0, 0], ycorner[0, 1])
        unpack(H + cx + x, ycorner[1, 0], ycorner[1, 1])
    for copy, _, can in passed:
        pl.when(can)(copy.wait_recv)
    smooth_z(nbuf.at[0], 0)
    smooth_z(nbuf.at[1], 2 * cx)
    for x in range(X0):
        smoothed = float(taper_weights[4]) * dens[x + 4]
        for k in range(1, 5):
            smoothed = smoothed + float(taper_weights[4 + k]) * (dens[x + 4 - k] + dens[x + 4 + k])
        shading = jnp.exp(-smoothed / density_scale)
        keep = keep_y
        if x < H:
            keep = keep_y * keep_left
        elif x >= H + cx:
            keep = keep_y * keep_right
        d0[x] = keep * (2.0 + 78.0 * shading)
        rb[x] = screening * shading * shading * opened[x]

    def weights(at, rows, wx, wyp, wym, wzp, wzm, face, scale):
        for x in rows:
            v = at(x)
            z, w = v.shape
            zrow = iota((z, w), 0)
            if x == rows[0]:
                wx[x] = (0.5 * scale) * (at(x - 1) + v)
            wx[x + 1] = (0.5 * scale) * (v + at(x + 1))
            yp = (0.5 * scale) * (v + pltpu.roll(v, w - 1, 1))
            ym = (0.5 * scale) * (v + pltpu.roll(v, 1, 1))
            zp = jnp.where(zrow == z - 1, 0.0, (0.5 * scale) * (v + pltpu.roll(v, z - 1, 0)))
            zm = jnp.where(zrow == 0, 0.0, (0.5 * scale) * (v + pltpu.roll(v, 1, 0)))
            wyp[x], wym[x], wzp[x], wzm[x] = yp, ym, zp, zm
            ends = jnp.where((zrow == 0) | (zrow == z - 1), (0.5 * scale) * v, 0.0)
            face[x] = wx[x] + wx[x + 1] + yp + ym + zp + zm + ends

    def around(v, x, wx, wyp, wym, wzp, wzm, shift=0):
        here = v[x + shift]
        z, w = here.shape
        return (
            (wx[x + 1] * v[x + shift + 1] + wx[x] * v[x + shift - 1])
            + (wzp[x] * pltpu.roll(here, z - 1, 0) + wzm[x] * pltpu.roll(here, 1, 0))
            + (wyp[x] * pltpu.roll(here, w - 1, 1) + wym[x] * pltpu.roll(here, 1, 1))
        )

    def d0_at(x):
        return d_far[0] if x < 0 else d_far[1] if x >= X0 else d0[x]

    def both_ways(slot, to_right, to_left):
        return [
            (remote(to_right[0], to_right[1], e_send.at[slot, 0], e_recv.at[slot, 0], right), has_right, has_left),
            (remote(to_left[0], to_left[1], e_send.at[slot, 1], e_recv.at[slot, 1], left), has_left, has_right),
        ]

    level0 = (wx, wyp, wym, wzp, wzm)
    level1 = (w1x, w1yp, w1ym, w1zp, w1zm)

    def coarse_row(a, c, slot):
        both = a + c
        lane = iota((z1, 128), 1)
        parts = []
        for i in range(3):
            tmp[slot, i] = both[:, i * 128 : (i + 1) * 128]
            parts.append(halved(
                tmp[slot, i, pl.ds(0, z1, stride=2), :] + tmp[slot, i, pl.ds(1, z1, stride=2), :], even
            ))
        return 0.125 * jnp.concatenate([jnp.where(lane < 64, parts[0], parts[1]), parts[2]], axis=1)

    def fine_row(c, slot):
        for i, index in enumerate((half, half_up, half_split)):
            wide = lanes_at(c[:, 128 * (i // 2) : 128 * (i // 2) + 128], index)
            tmp[slot, i, pl.ds(0, z1, stride=2), :] = wide
            tmp[slot, i, pl.ds(1, z1, stride=2), :] = wide
        return jnp.concatenate([tmp[slot, i] for i in range(3)], axis=1)

    def message(f, slot):
        for k in range(2):
            tmp1[slot, k * z1 : (k + 1) * z1, :] = f(H + 2 * k) + f(H + 2 * k + 1)
        w = tmp1[slot, pl.ds(0, mrows, stride=2), :] + tmp1[slot, pl.ds(1, mrows, stride=2), :]
        return 0.125 * halved(w, even)

    def safe_step(d, diagonal):
        return jnp.where(d > 0.0, damping / diagonal, 0.0)

    def gather_send(n, own, side, got, gots):
        for k in range(bulks - 1, 0, -1):
            remote(own, got.at[b], g_send.at[n, 2], g_recv.at[n, 2], (s, flip(b, k))).start()
        for i, (can, row) in enumerate(((has_high, s + 1), (has_low, s - 1))):
            @pl.when(can)
            def _():
                for k in range(bulks - 1, -1, -1):
                    remote(
                        side.at[i], gots.at[i, b], g_send.at[n, i], g_recv.at[n, i],
                        (row, flip(b, k) if k else b),
                    ).start()

    def gather_copy(n, got, gots, i):
        part = got.at[0 : bulks - 1] if i == 2 else gots.at[i]
        return remote(part, part, g_send.at[n, i], g_recv.at[n, i], (s, flip(b, 1)))

    def gather_wait(n, got, gots):
        gather_copy(n, got, gots, 2).wait_recv()
        pl.when(has_low)(gather_copy(n, got, gots, 0).wait_recv)
        pl.when(has_high)(gather_copy(n, got, gots, 1).wait_recv)

    def gather_drain(n, got, gots):
        gather_copy(n, got, gots, 2).wait_send()
        pl.when(has_high)(gather_copy(n, got, gots, 0).wait_send)
        pl.when(has_low)(gather_copy(n, got, gots, 1).wait_send)

    def flat_weights(w_ref, d, z, scale):
        rows = d.shape[0]
        row = iota(d.shape, 0)
        zrow = row & (z - 1)
        total = None
        for i, (outside, other) in enumerate((
            (row < z, pltpu.roll(d, z, 0)), (row >= rows - z, pltpu.roll(d, rows - z, 0)),
            (zrow == 0, pltpu.roll(d, 1, 0)), (zrow == z - 1, pltpu.roll(d, rows - 1, 0)),
            (None, pltpu.roll(d, 1, 1)), (None, pltpu.roll(d, 127, 1)),
        )):
            w = (0.5 * scale) * (d + other)
            if outside is None:
                w_ref[i] = w
            else:
                w_ref[i] = jnp.where(outside, 0.0, w)
                w = jnp.where(outside, (0.5 * scale) * d, w)
            total = w if total is None else total + w
        return total

    def flat_around(w_ref, v, z):
        rows = v.shape[0]
        return (
            (w_ref[4] * pltpu.roll(v, 1, 1) + w_ref[5] * pltpu.roll(v, 127, 1))
            + ((w_ref[0] * pltpu.roll(v, z, 0) + w_ref[1] * pltpu.roll(v, rows - z, 0))
               + (w_ref[2] * pltpu.roll(v, 1, 0) + w_ref[3] * pltpu.roll(v, rows - 1, 0)))
        )

    def flat_coarse(v, z, slot):
        rows = v.shape[0]
        tmp3[slot] = v
        w = tmp3[slot, pl.ds(0, rows // 2, stride=2), :] + tmp3[slot, pl.ds(1, rows // 2, stride=2), :]
        zc = z // 2
        pieces = [w[(2 * k) * zc : (2 * k + 1) * zc] + w[(2 * k + 1) * zc : (2 * k + 2) * zc] for k in range(rows // (4 * zc))]
        return 0.125 * halved(jnp.concatenate(pieces, axis=0), even)

    def flat_fine(v, z):
        wide = lanes_at(v, half)
        zc = z // 2
        pieces = []
        for k in range(v.shape[0] // zc):
            pieces += [wide[k * zc : (k + 1) * zc]] * 2
        doubled = jnp.concatenate(pieces, axis=0)
        rows = 4 * v.shape[0]
        tmp3[0, pl.ds(0, rows // 2, stride=2), :] = doubled
        tmp3[0, pl.ds(1, rows // 2, stride=2), :] = doubled
        return tmp3[0]

    near1 = range(2, X1 - 2)

    def two(field, k):
        return field[2 * k - H], field[2 * k - H + 1]

    far = both_ways(0, (d0.at[H + 3], d_far.at[0]), (d0.at[H + cx - 4], d_far.at[1]))
    for copy, can, _ in far:
        go(copy, can)
    weights(d0_at, range(1, X0 - 1), *level0, face, 1.0)
    for k in near1:
        d1[k] = coarse_row(*two(d0, k), k)
    copies = both_ways(1, (d1.at[H : H + 2], d1.at[0:2]), (d1.at[H + 2 : H + 4], d1.at[X1 - 2 : X1]))
    for copy, can, _ in copies:
        go(copy, can)
    far += copies
    weights(lambda k: d1[k], near1[1:-1], *level1, face1, 0.25)
    face2 = face3 = None
    d2 = None

    for n in range(NEWTON):
        inner = range(1, X0 - 1)
        if n == 0:
            target, c_of = src, rb
        else:
            target, c_of = tgt, c0

            def reaction(x):
                sh, ch = sinh_cosh(pot[x])
                c0[x] = rb[x] * ch
                if x in inner:
                    tgt[x] = src[x] - rb[x] * sh
                    return True

            def misfit_row(x):
                tgt[x] = tgt[x] - face[x] * pot[x] + around(pot, x, *level0)

            for x in range(X0):
                reaction(x)
            for x in inner:
                misfit_row(x)
        for x in inner:
            st = safe_step(d0[x], face[x] + c_of[x])
            step0[x] = st
            v0[x] = st * target[x]
        if n == 0:
            beside = both_ways(3, (v0.at[H + 3], v_far.at[0]), (v0.at[H + cx - 4], v_far.at[1]))
            for copy, can, _ in beside:
                pl.when(can)(copy.start)
        for k in near1:
            c1[k] = coarse_row(*two(c_of, k), k)
        held = []
        if n == 0:
            held += beside
            copies = both_ways(2, (c1.at[H + 1], c1.at[1]), (c1.at[H + 2], c1.at[X1 - 2]))
            for copy, can, _ in copies:
                pl.when(can)(copy.start)
            far += copies
            held += copies

        def residual0(x):
            return rest * target[x] + around(v0, x, *level0)

        for k in near1[1:-1]:
            t1[k] = coarse_row(residual0(2 * k - H), residual0(2 * k - H + 1), X1 + k)
        for k in near1[1:-1]:
            st = safe_step(d1[k], face1[k] + c1[k])
            step1[k] = st
            v1[k] = st * t1[k]
        if n == 0:
            copies = both_ways(4, (v1.at[H], v1.at[0]), (v1.at[H + 3], v1.at[X1 - 1]))
            copies += both_ways(5, (t1.at[H + 1 : H + 3], t1.at[1:3]), (t1.at[H + 1 : H + 3], t1.at[X1 - 3 : X1 - 1]))
            beside += copies
        else:
            beside = copies = both_ways(6, (v1.at[H + 2], hv1.at[0]), (v1.at[H + 1], hv1.at[1]))
        for copy, can, _ in copies:
            pl.when(can)(copy.start)
        held += copies

        def residual1(k):
            return rest * t1[k, :, 0:128] + around(v1, k, *level1)[:, 0:128]

        t2_own = message(residual1, 0)
        c2_own = message(lambda k: c1[k, :, 0:128], 1)
        lane_m = iota((mrows, 128), 1)
        own, side, got, gots = (own0, side0, got0, gots0) if n == 0 else (own1, side1, got1, gots1)
        own[0:mrows] = jnp.where(lane_m < 64, t2_own, c2_own)
        to_high = jnp.where(lane_m < 64, c2_own, t2_own)
        to_low = to_high
        if n == 0:
            d2_own = message(lambda k: d1[k, :, 0:128], 2)
            own[mrows : 2 * mrows] = d2_own
            moved = pltpu.roll(d2_own, 32, 1)
            to_high = jnp.where(lane_m >> 5 == 2, moved, to_high)
            to_low = jnp.where(lane_m >> 5 == 3, moved, to_low)
        side[0], side[1] = to_high, to_low
        gather_send(n, own, side, got, gots)
        got[b] = own[...]
        if n == 0:
            for copy, _, can in far:
                pl.when(can)(copy.wait_recv)
            for x in (0, X0 - 1):
                weights(d0_at, range(x, x + 1), *level0, face, 1.0)
                st = safe_step(d0[x], face[x] + rb[x])
                step0[x] = st
                v0[x] = st * src[x]
            for rows in (range(1, 3), range(X1 - 3, X1 - 1)):
                weights(lambda k: d1[k], rows, *level1, face1, 0.25)
                for k in rows:
                    step1[k] = safe_step(d1[k], face1[k] + c1[k])
        gather_wait(n, got, gots)
        lane2 = iota((rows2, 128), 1)
        mine2, low2, high2 = [ref.reshape(rows2, 128) for ref in (got[:, 0:mrows], gots[0], gots[1])]
        t2 = jnp.where(lane2 < 64, mine2, jnp.where(lane2 < 96, high2, low2))
        c2 = pltpu.roll(jnp.where(lane2 >= 64, mine2, jnp.where(lane2 < 32, high2, low2)), 64, 1)
        if n == 0:
            d2 = jnp.where(
                lane2 < 64, got[:, mrows : 2 * mrows].reshape(rows2, 128),
                jnp.where(lane2 < 96, pltpu.roll(high2, 96, 1), pltpu.roll(low2, 32, 1)),
            )
            d3 = flat_coarse(d2, z2, 2)
            face2 = flat_weights(w2, d2, z2, 0.25**2)
            face3 = flat_weights(w3, d3, z3, 0.25**3)
        step2 = safe_step(d2, face2 + c2)
        v2 = step2 * t2
        t3 = flat_coarse(rest * t2 + flat_around(w2, v2, z2), z2, 0)
        c3 = flat_coarse(c2, z2, 1)
        step3 = safe_step(d3, face3 + c3)
        v3 = step3 * t3
        base = v3
        for repeat in range(COARSE - 1):
            v3 = (rest * v3 + base) + step3 * flat_around(w3, v3, z3)
        v2 = v2 + flat_fine(v3, z2)
        v2 = (rest * v2 + step2 * t2) + step2 * flat_around(w2, v2, z2)
        v2_ref[0:mrows] = jnp.zeros((mrows, 128), f32)
        v2_ref[mrows : mrows + rows2] = v2
        v2_ref[mrows + rows2 :] = jnp.zeros((mrows, 128), f32)
        near = v2_ref[pl.ds(pl.multiple_of(b * mrows, 8), 3 * mrows), :]
        for i, index in enumerate((half, half_up)):
            wide = lanes_at(near, index)
            e_ref[i, pl.ds(0, 3 * mrows, stride=2), :] = wide
            e_ref[i, pl.ds(1, 3 * mrows, stride=2), :] = wide
        for copy, _, can in beside:
            pl.when(can)(copy.wait_recv)
        wide1 = range(X1) if n == 0 else near1
        wide0 = range(-1, X0 + 1) if n == 0 else range(H - 2, H + cx + 2)
        if n == 0:
            for k in (1, 2, X1 - 3, X1 - 2):
                v1[k] = step1[k] * t1[k]
        for k in wide1:
            before = v1[k]
            if n == 1 and k in (near1[0], near1[-1]):
                before = hv1[0 if k == near1[0] else 1]
            at = (k // 2) * z1
            tmp2[k] = before + jnp.concatenate([e_ref[i, at : at + z1, :] for i in range(2)], axis=1)
        for k in wide1[1:-1]:
            better = rest * tmp2[k] + step1[k] * (t1[k] + around(tmp2, k, *level1))
            fine = fine_row(better, k)
            for x in (2 * k - H, 2 * k - H + 1):
                if x in wide0:
                    vb[x + 1] = (v_far[0] if x < 0 else v_far[1] if x >= X0 else v0[x]) + fine
        for x in wide0[1:-1]:
            new = rest * vb[x + 1] + step0[x] * (target[x] + around(vb, x, *level0, shift=1))
            if n == 0:
                pot[x] = new
            else:
                pot2[x] = pot[x] + new
        for copy, can, _ in held:
            pl.when(can)(copy.wait_send)

    zrow = iota((z0, y), 0)
    end = (zrow == 0) | (zrow == z0 - 1)
    for x in range(H, H + cx):
        here = pot2[x]
        mid = here[:, 0:y]
        for i in range(2):
            turned[0, i, pl.ds(x - H, nz, stride=cx), :] = mid[:, i * 128 : (i + 1) * 128]
        sh, _ = sinh_cosh(mid)
        total = wx[x + 1, :, 0:y] * (mid - pot2[x + 1, :, 0:y]) + wx[x, :, 0:y] * (mid - pot2[x - 1, :, 0:y])
        total = total + wzp[x, :, 0:y] * (mid - pltpu.roll(mid, z0 - 1, 0)) + wzm[x, :, 0:y] * (mid - pltpu.roll(mid, 1, 0))
        total = total + wyp[x, :, 0:y] * (mid - pltpu.roll(here, W0 - 1, 1)[:, 0:y])
        total = total + wym[x, :, 0:y] * (mid - pltpu.roll(here, 1, 1)[:, 0:y])
        total = total + jnp.where(end, 0.5 * d0[x, :, 0:y], 0.0) * mid
        total = total + rb[x, :, 0:y] * sh - src[x, :, 0:y]
        for i in range(2):
            turned[1, i, pl.ds(x - H, nz, stride=cx), :] = total[:, i * 128 : (i + 1) * 128]
    for i in range(2):
        pot_out[:, i * 128 : (i + 1) * 128] = turned[0, i]
        mis_out[:, i * 128 : (i + 1) * 128] = turned[1, i]

    for out, _ in slab_copies:
        out.wait_send()
    for copy, can in sent:
        pl.when(can)(copy.wait_send)
    gather_drain(0, got0, gots0)
    gather_drain(1, got1, gots1)


def written(pot, mis, pot_out, mis_out, sem):
    copies = [pltpu.make_async_copy(pot, pot_out, sem.at[0]), pltpu.make_async_copy(mis, mis_out, sem.at[1])]
    for copy in copies:
        copy.start()
    for copy in copies:
        copy.wait()


def per_device(atom_counts, ion_flags, charge_cells, charge_values):
    slabs, bulks = lax.axis_size("slab"), lax.axis_size("bulk")
    nz, cx, y = ion_flags.shape
    z1, z2, z3 = nz // 2, nz // 4, nz // 8
    X0, X1 = cx + 2 * H, cx // 2 + 2 * H
    W0, W1 = y + 128, y // 2 + 128
    arows = nz * cx // slabs
    piece = 2 * arows + cx
    mrows = 2 * z2
    rows2, rows3 = bulks * mrows, bulks * z3
    i32 = jnp.int32
    vm = pltpu.VMEM
    dma = pltpu.SemaphoreType.DMA

    def level0(n=X0):
        return vm((n, nz, W0), f32)

    def level1(n=X1):
        return vm((n, z1, W1), f32)

    pot, mis = pl.pallas_call(
        lambda *refs: solver(slabs, bulks, nz, cx, y, *refs),
        out_shape=[jax.ShapeDtypeStruct((nz * cx, y), f32)] * 2,
        in_specs=[pl.BlockSpec(memory_space=pl.ANY)] * 4,
        out_specs=[pl.BlockSpec(memory_space=pltpu.VMEM)] * 2,
        scratch_shapes=[
            vm(atom_counts.shape, i32), vm((2, nz * cx, 128), i32),
            vm((1,) + charge_cells.shape, i32), vm((1,) + charge_values.shape, f32),
            vm((slabs, piece, 128), f32), vm((slabs, piece, 128), f32), vm((2, slabs, piece, 128), f32),
            level0(3 * cx), level0(), level0(),
            vm((2, 2, nz, 128), f32), vm((2, 2, nz, 128), f32), vm((2, 2, nz, 128), f32),
            level0(), level0(2), level0(), level0(X0 + 1), level0(), level0(), level0(), level0(), level0(), level0(),
            level0(), level0(), level0(2), level0(X0 + 2), level0(), level0(), level0(), vm((2 * X1, 3, nz, 128), f32),
            level1(), level1(X1 + 1), level1(), level1(), level1(), level1(), level1(), level1(), level1(), level1(),
            level1(), level1(2), vm((3, 2 * z1, 128), f32), level1(),
            vm((2 * mrows, 128), f32), vm((mrows, 128), f32), vm((2, mrows, 128), f32), vm((2, mrows, 128), f32),
            vm((bulks, 2 * mrows, 128), f32), vm((bulks, mrows, 128), f32),
            vm((2, bulks, mrows, 128), f32), vm((2, bulks, mrows, 128), f32),
            vm((6, rows2, 128), f32), vm((6, rows3, 128), f32),
            vm((rows2 + 2 * mrows, 128), f32), vm((2, 6 * mrows, 128), f32), vm((3, rows2, 128), f32),
            vm((2, 2, nz * cx, 128), f32),
            dma((5,)), dma((slabs,)), dma((slabs,)), dma((slabs, 2)), dma((slabs, 2)),
            dma((3, 2)), dma((3, 2)), dma((2,)), dma((2,)),
            dma((7, 2)), dma((7, 2)), dma((2, 3)), dma((2, 3)),
        ],
        compiler_params=pltpu.CompilerParams(
            collective_id=0, has_side_effects=True, vmem_limit_bytes=40 << 20
        ),
    )(*[
        pltpu.with_memory_space_constraint(field, pltpu.HBM)
        for field in (atom_counts, ion_flags.reshape(nz * cx, y), charge_cells[None], charge_values[None])
    ])
    pot, mis = pl.pallas_call(
        written,
        out_shape=[jax.ShapeDtypeStruct((nz * cx, y), f32)] * 2,
        in_specs=[pl.BlockSpec(memory_space=pl.ANY)] * 2,
        out_specs=[pl.BlockSpec(memory_space=pl.ANY)] * 2,
        scratch_shapes=[dma((2,))],
        compiler_params=pltpu.CompilerParams(vmem_limit_bytes=1 << 20),
    )(pot, mis)
    return pot.reshape(nz, cx, y), mis.reshape(nz, cx, y)


def solution(mesh):
    placed = (
        P("slab", "bulk", None),
        P(None, "bulk", "slab"),
        P(("slab", "bulk")),
        P(("slab", "bulk")),
    )
    return jax.shard_map(
        per_device,
        mesh=mesh,
        in_specs=placed,
        out_specs=(P(None, "bulk", "slab"), P(None, "bulk", "slab")),
        check_vma=False,
    )
```

```python
import jax
import jax.numpy as jnp
import numpy as np
from jax import lax
from jax.experimental import pallas as pl
from jax.experimental.pallas import tpu as pltpu
from jax.sharding import PartitionSpec as P

COARSE = 8
NEWTON = 2
ROUND = 2
H = 4

taper_raw = np.exp(-0.5 * (np.arange(-4, 5) / 1.5) ** 2)
taper_weights = taper_raw / taper_raw.sum()
damping = 0.8
rest = 1.0 - damping
screening = 1.0
density_scale = 2.0

MESH_ID = pl.DeviceIdType.MESH
LN2 = float(np.log(2.0))
f32 = jnp.float32


def iota(shape, dim):
    return lax.broadcasted_iota(jnp.int32, shape, dim)


def log2(n):
    return int(n).bit_length() - 1


def mm(a, b):
    return lax.dot_general(
        a, b, (((1,), (0,)), ((), ())),
        precision=lax.Precision.HIGHEST, preferred_element_type=f32,
    )


def sinh_cosh(p):
    a, b = jnp.exp(p - LN2), jnp.exp(-p - LN2)
    q = jnp.minimum(p * p, 1.0)
    small = p * (
        1.0
        + q * (1 / 6) * (1.0 + q * (1 / 20) * (1.0 + q * (1 / 42) * (1.0 + q * (1 / 72) * (1.0 + q * (1 / 110)))))
    )
    return jnp.where(jnp.abs(p) < 1.0, small, a - b), a + b


def taper_y(density):
    width = density.shape[1]
    lane = iota(density.shape, 1)
    summed = float(taper_weights[4]) * density
    for k in range(1, 5):
        before = jnp.where(lane < k, 0.0, pltpu.roll(density, k, 1))
        after = jnp.where(lane >= width - k, 0.0, pltpu.roll(density, width - k, 1))
        summed = summed + float(taper_weights[4 + k]) * (before + after)
    return summed


def taper_z(rows, z, cx):
    i, j = iota((rows, rows), 0), iota((rows, rows), 1)
    far = jnp.abs((i & (z - 1)) - (j >> log2(cx)))
    band = jnp.zeros((rows, rows), f32)
    for k in range(5):
        band = jnp.where(far == k, float(taper_weights[4 + k]), band)
    return jnp.where((i >> log2(z)) == (j & (cx - 1)), band, 0.0)


def scattered(cells, values, rows, z, cx, y):
    entries = cells.shape[1]
    ly, lx = log2(y), log2(cx)
    row = ((cells >> ly) & (cx - 1)) * z + (cells >> (ly + lx))
    at_row = jnp.where(iota((rows, entries), 0) == row, values, 0.0)
    at_y = jnp.where(iota((y, entries), 0) == (cells & (y - 1)), f32(1.0), f32(0.0))
    return lax.dot_general(
        at_row, at_y, (((1,), (1,)), ((), ())),
        precision=lax.Precision.HIGHEST, preferred_element_type=f32,
    )


def lanes_at(v, index):
    parts = [
        jnp.take_along_axis(v[i : i + 8], index, axis=1, mode="promise_in_bounds")
        for i in range(0, v.shape[0], 8)
    ]
    return parts[0] if len(parts) == 1 else jnp.concatenate(parts, axis=0)


def halved(v, index):
    return lanes_at(v + pltpu.roll(v, 127, 1), index)


def solver(
    slabs, bulks, nz, cx, y,
    atoms_hbm, flags_hbm, cells_hbm, values_hbm, pot_out, mis_out,
    atoms_in, flags_in, cells_in, values_in,
    ay, abuf, nbuf, dens, opened, src, yout, yin, ycorner,
    d0, d_far, rb, wx, wyp, wym, wzp, wzm, face, c0, step0, v0, v_far, vb, tgt, pot, pot2, tmp,
    d1, w1x, w1yp, w1ym, w1zp, w1zm, face1, c1, step1, t1, v1, hv1, tmp1, tmp2,
    own0, own1, side0, side1, got0, got1, gots0, gots1, w2, w3, v2_ref, e_ref, tmp3, tmp4, turned,
    load_sem, a_send, a_recv, f_send, f_recv, x_send, x_recv, y_send, y_recv,
    e_send, e_recv, g_send, g_recv,
):
    s, b = lax.axis_index("slab"), lax.axis_index("bulk")
    z0, z1, z2, z3 = nz, nz // 2, nz // 4, nz // 8
    X0, X1 = cx + 2 * H, cx // 2 + 2 * H
    W0, W1 = y + 128, y // 2 + 128
    mrows = 2 * z2
    rows2, rows3 = bulks * mrows, bulks * z3
    at_left, at_right = b == 0, b == bulks - 1
    at_low, at_high = s == 0, s == slabs - 1
    has_left, has_right = b > 0, b < bulks - 1
    has_low, has_high = s > 0, s < slabs - 1

    loads = [
        pltpu.make_async_copy(there, here, load_sem.at[i])
        for i, (there, here) in enumerate((
            (atoms_hbm, atoms_in), (cells_hbm, cells_in), (values_hbm, values_in),
            (flags_hbm.at[:, 0:128], flags_in.at[0]), (flags_hbm.at[:, 128:256], flags_in.at[1]),
        ))
    ]
    for load in loads:
        load.start()

    def flip(at, k):
        for i in range(log2(k) + 1):
            if k >> i & 1:
                at = at + (1 << i) * (1 - 2 * (at // (1 << i) % 2))
        return at

    barrier = pltpu.get_barrier_semaphore()
    for k in range(1, slabs):
        pl.semaphore_signal(barrier, inc=1, device_id=(flip(s, k), b), device_id_type=MESH_ID)
    for k in range(1, bulks):
        pl.semaphore_signal(barrier, inc=1, device_id=(s, flip(b, k)), device_id_type=MESH_ID)

    def clear(*refs):
        for ref in refs:
            ref[...] = jnp.zeros(ref.shape, ref.dtype)

    @pl.when(at_left)
    def _():
        clear(nbuf.at[0], opened.at[0:H], src.at[0:H], ycorner.at[0], hv1.at[0], d_far.at[0], v_far.at[0],
              d1.at[0:2], c1.at[1], t1.at[1:3], v1.at[0])

    @pl.when(at_right)
    def _():
        clear(
            nbuf.at[1], opened.at[H + cx : X0], src.at[H + cx : X0], ycorner.at[1],
            hv1.at[1], d_far.at[1], v_far.at[1], d1.at[X1 - 2 : X1], c1.at[X1 - 2], t1.at[X1 - 3 : X1 - 1], v1.at[X1 - 1],
        )

    @pl.when(at_low)
    def _():
        clear(gots0.at[0], gots1.at[0], yin.at[0])

    @pl.when(at_high)
    def _():
        clear(gots0.at[1], gots1.at[1], yin.at[1])

    def remote(source, target, send, recv, to):
        return pltpu.make_async_remote_copy(
            src_ref=source, dst_ref=target, send_sem=send, recv_sem=recv,
            device_id=to, device_id_type=MESH_ID,
        )

    right, left = (s, b + 1), (s, b - 1)
    high, low = (s + 1, b), (s - 1, b)
    sent = []

    def go(copy, can):
        pl.when(can)(copy.start)
        sent.append((copy, can))

    loads[0].wait()
    smooth_y = taper_y(atoms_in[...].astype(f32).reshape(-1, slabs * y))
    arows = smooth_y.shape[0]
    planes = arows // cx
    lane_a = iota((arows, 128), 1)
    lane_c = iota((cx, 128), 1)
    nothing = jnp.zeros((arows, 128), f32)
    for t in range(slabs):
        for i in range(2):
            ay[t, i * arows : (i + 1) * arows] = smooth_y[:, t * y + i * 128 : t * y + (i + 1) * 128]
        after = smooth_y[:, (t + 1) * y : (t + 1) * y + 128] if t < slabs - 1 else nothing
        before = smooth_y[:, t * y - 128 : t * y] if t else nothing
        beside = jnp.where(lane_a < 64, after, before)
        packed = beside[0:cx]
        for g in range(1, planes):
            moved = pltpu.roll(beside[g * cx : (g + 1) * cx], 32 * g, 1)
            packed = jnp.where((((lane_c + 16) >> 5) & 3) == g, moved, packed)
        ay[t, 2 * arows :] = packed

    slab_copies = [
        (remote(ay.at[flip(s, k)], abuf.at[s], a_send.at[k], a_recv.at[k], (flip(s, k), b)),
         remote(ay.at[flip(s, k)], abuf.at[flip(s, k)], a_send.at[k], a_recv.at[k], (flip(s, k), b)))
        for k in range(1, slabs)
    ]
    pl.semaphore_wait(barrier, slabs + bulks - 2)
    for out, _ in slab_copies:
        out.start()

    def pass_on(k):
        which = flip(s, k) if k else s
        return [
            (remote(abuf.at[which], nbuf.at[0, which], f_send.at[k, 0], f_recv.at[k, 0], right), has_right, has_left),
            (remote(abuf.at[which], nbuf.at[1, which], f_send.at[k, 1], f_recv.at[k, 1], left), has_left, has_right),
        ]

    passed = []
    abuf[s] = ay[s]
    passed += pass_on(0)
    for copy, can, _ in passed:
        go(copy, can)

    def rows_both_ways(source, target, slot, lanes):
        return [
            (remote(
                source.at[cx : cx + H, :, lanes], target.at[0:H, :, lanes],
                x_send.at[slot, 0], x_recv.at[slot, 0], right,
            ), has_right, has_left),
            (remote(
                source.at[H : 2 * H, :, lanes], target.at[H + cx : X0, :, lanes],
                x_send.at[slot, 1], x_recv.at[slot, 1], left,
            ), has_left, has_right),
        ]

    for load in loads[1:]:
        load.wait()
    for x in range(cx):
        for i in range(2):
            flags = flags_in[i, pl.ds(x, nz, stride=cx), :]
            opened[H + x, :, i * 128 : (i + 1) * 128] = 1.0 - flags.astype(f32)
    x_copies = rows_both_ways(opened, opened, 0, slice(0, y))
    for copy, can, _ in x_copies:
        go(copy, can)
    charges = scattered(cells_in[...], values_in[...], cx * z0, z0, cx, y)
    for x in range(cx):
        src[H + x, :, 0:y] = charges[x * z0 : (x + 1) * z0]
    copies = rows_both_ways(src, src, 1, slice(0, y))
    for copy, can, _ in copies:
        go(copy, can)
    x_copies += copies

    lane_h = iota((z0, 128), 1)
    for q in range(2):
        to_high = to_low = jnp.zeros((z0, 128), f32)
        for j in range(8):
            field = (opened, src)[j // 4]
            x = H + 4 * q + j % 4
            to_high = jnp.where(lane_h >> 4 == j, pltpu.roll(field[x, :, y - 128 : y], (16 * j + 16) % 128, 1), to_high)
            to_low = jnp.where(lane_h >> 4 == (j + 1) % 8, pltpu.roll(field[x, :, 0:128], (16 * j + 16) % 128, 1), to_low)
        yout[0, q], yout[1, q] = to_high, to_low
    y_copies = [
        (remote(yout.at[0], yin.at[0], y_send.at[0], y_recv.at[0], high), has_high, has_low),
        (remote(yout.at[1], yin.at[1], y_send.at[1], y_recv.at[1], low), has_low, has_high),
    ]
    for copy, can, _ in y_copies:
        go(copy, can)
    corner_copies = [
        (remote(yin.at[:, 1], ycorner.at[0], x_send.at[2, 0], x_recv.at[2, 0], right), has_right, has_left),
        (remote(yin.at[:, 0], ycorner.at[1], x_send.at[2, 1], x_recv.at[2, 1], left), has_left, has_right),
    ]

    along_z = taper_z(cx * z0, z0, cx)
    for k in range(1, slabs):
        slab_copies[k - 1][1].wait_recv()
        copies = pass_on(k)
        for copy, can, _ in copies:
            go(copy, can)
        passed += copies

    def smooth_z(pieces, at):
        columns = [pieces[:, i * arows : (i + 1) * arows].reshape(cx * z0, 128) for i in range(2)]
        edges = []
        for t in range(slabs):
            packed = pieces[t, 2 * arows :]
            edges += [packed] + [pltpu.roll(packed, 128 - 32 * g, 1) for g in range(1, planes)]
        columns.append(jnp.concatenate(edges, axis=0))
        for i, column in enumerate(columns):
            dens[at : at + cx, :, i * 128 : (i + 1) * 128] = mm(along_z, column).reshape(cx, z0, 128)

    for copy, _, can in y_copies:
        pl.when(can)(copy.wait_recv)
    for copy, can, _ in corner_copies:
        go(copy, can)
    smooth_z(abuf, cx)

    def unpack(x, from_low, from_high):
        for a, field in enumerate((opened, src)):
            j = 4 * a + x % 4
            both = jnp.where(lane_h >> 4 == j, from_low, from_high)
            both = pltpu.roll(both, (112 - 16 * j) % 128, 1)
            field[x, :, y:W0] = jnp.where((lane_h < 16) | (lane_h >= 112), both, 0.0)

    for x in range(H, H + cx):
        unpack(x, yin[0, x // 4 - 1], yin[1, x // 4 - 1])
    lane0 = iota((z0, W0), 1)
    keep_low = jnp.where(at_low, f32(0.0), f32(1.0))
    keep_high = jnp.where(at_high, f32(0.0), f32(1.0))
    keep_y = jnp.where(lane0 < y, 1.0, jnp.where(lane0 < y + 64, keep_high, keep_low))
    keep_left = jnp.where(at_left, f32(0.0), f32(1.0))
    keep_right = jnp.where(at_right, f32(0.0), f32(1.0))
    zrow0 = iota((z0, W0), 0)
    lane128 = iota((8, 128), 1)
    even = (2 * lane128) & 127
    half = lane128 >> 1
    half_up = 64 + half
    half_split = jnp.where(lane128 < 64, half, half_up)

    for copy, _, can in x_copies + corner_copies:
        pl.when(can)(copy.wait_recv)
    for x in range(H):
        unpack(x, ycorner[0, 0], ycorner[0, 1])
        unpack(H + cx + x, ycorner[1, 0], ycorner[1, 1])
    for copy, _, can in passed:
        pl.when(can)(copy.wait_recv)
    smooth_z(nbuf.at[0], 0)
    smooth_z(nbuf.at[1], 2 * cx)
    for x in range(X0):
        smoothed = float(taper_weights[4]) * dens[x + 4]
        for k in range(1, 5):
            smoothed = smoothed + float(taper_weights[4 + k]) * (dens[x + 4 - k] + dens[x + 4 + k])
        shading = jnp.exp(-smoothed / density_scale)
        keep = keep_y
        if x < H:
            keep = keep_y * keep_left
        elif x >= H + cx:
            keep = keep_y * keep_right
        d0[x] = keep * (2.0 + 78.0 * shading)
        rb[x] = screening * shading * shading * opened[x]

    def weights(at, rows, wx, wyp, wym, wzp, wzm, face, scale):
        for x in rows:
            v = at(x)
            z, w = v.shape
            zrow = iota((z, w), 0)
            if x == rows[0]:
                wx[x] = (0.5 * scale) * (at(x - 1) + v)
            wx[x + 1] = (0.5 * scale) * (v + at(x + 1))
            yp = (0.5 * scale) * (v + pltpu.roll(v, w - 1, 1))
            ym = (0.5 * scale) * (v + pltpu.roll(v, 1, 1))
            zp = jnp.where(zrow == z - 1, 0.0, (0.5 * scale) * (v + pltpu.roll(v, z - 1, 0)))
            zm = jnp.where(zrow == 0, 0.0, (0.5 * scale) * (v + pltpu.roll(v, 1, 0)))
            wyp[x], wym[x], wzp[x], wzm[x] = yp, ym, zp, zm
            ends = jnp.where((zrow == 0) | (zrow == z - 1), (0.5 * scale) * v, 0.0)
            face[x] = wx[x] + wx[x + 1] + yp + ym + zp + zm + ends

    def around(v, x, wx, wyp, wym, wzp, wzm, shift=0):
        here = v[x + shift]
        z, w = here.shape
        return (
            (wx[x + 1] * v[x + shift + 1] + wx[x] * v[x + shift - 1])
            + (wzp[x] * pltpu.roll(here, z - 1, 0) + wzm[x] * pltpu.roll(here, 1, 0))
            + (wyp[x] * pltpu.roll(here, w - 1, 1) + wym[x] * pltpu.roll(here, 1, 1))
        )

    def d0_at(x):
        return d_far[0] if x < 0 else d_far[1] if x >= X0 else d0[x]

    def both_ways(slot, to_right, to_left):
        return [
            (remote(to_right[0], to_right[1], e_send.at[slot, 0], e_recv.at[slot, 0], right), has_right, has_left),
            (remote(to_left[0], to_left[1], e_send.at[slot, 1], e_recv.at[slot, 1], left), has_left, has_right),
        ]

    level0 = (wx, wyp, wym, wzp, wzm)
    level1 = (w1x, w1yp, w1ym, w1zp, w1zm)

    def coarse_row(a, c, slot):
        both = a + c
        lane = iota((z1, 128), 1)
        parts = []
        for i in range(3):
            tmp[slot, i] = both[:, i * 128 : (i + 1) * 128]
            parts.append(halved(
                tmp[slot, i, pl.ds(0, z1, stride=2), :] + tmp[slot, i, pl.ds(1, z1, stride=2), :], even
            ))
        return 0.125 * jnp.concatenate([jnp.where(lane < 64, parts[0], parts[1]), parts[2]], axis=1)

    def fine_row(c, slot):
        for i, index in enumerate((half, half_up, half_split)):
            wide = lanes_at(c[:, 128 * (i // 2) : 128 * (i // 2) + 128], index)
            tmp[slot, i, pl.ds(0, z1, stride=2), :] = wide
            tmp[slot, i, pl.ds(1, z1, stride=2), :] = wide
        return jnp.concatenate([tmp[slot, i] for i in range(3)], axis=1)

    def message(f, slot):
        for k in range(2):
            tmp1[slot, k * z1 : (k + 1) * z1, :] = f(H + 2 * k) + f(H + 2 * k + 1)
        w = tmp1[slot, pl.ds(0, mrows, stride=2), :] + tmp1[slot, pl.ds(1, mrows, stride=2), :]
        return 0.125 * halved(w, even)

    def safe_step(d, diagonal):
        return jnp.where(d > 0.0, damping / diagonal, 0.0)

    def gather_send(n, own, side, got, gots):
        for k in range(bulks - 1, 0, -1):
            remote(own, got.at[b], g_send.at[n, 2], g_recv.at[n, 2], (s, flip(b, k))).start()
        for i, (can, row) in enumerate(((has_high, s + 1), (has_low, s - 1))):
            @pl.when(can)
            def _():
                for k in range(bulks - 1, -1, -1):
                    remote(
                        side.at[i], gots.at[i, b], g_send.at[n, i], g_recv.at[n, i],
                        (row, flip(b, k) if k else b),
                    ).start()

    def gather_copy(n, got, gots, i):
        part = got.at[0 : bulks - 1] if i == 2 else gots.at[i]
        return remote(part, part, g_send.at[n, i], g_recv.at[n, i], (s, flip(b, 1)))

    def gather_wait(n, got, gots):
        gather_copy(n, got, gots, 2).wait_recv()
        pl.when(has_low)(gather_copy(n, got, gots, 0).wait_recv)
        pl.when(has_high)(gather_copy(n, got, gots, 1).wait_recv)

    def gather_drain(n, got, gots):
        gather_copy(n, got, gots, 2).wait_send()
        pl.when(has_high)(gather_copy(n, got, gots, 0).wait_send)
        pl.when(has_low)(gather_copy(n, got, gots, 1).wait_send)

    def flat_weights(w_ref, d, z, scale):
        rows = d.shape[0]
        row = iota(d.shape, 0)
        zrow = row & (z - 1)
        total = None
        for i, (outside, other) in enumerate((
            (row < z, pltpu.roll(d, z, 0)), (row >= rows - z, pltpu.roll(d, rows - z, 0)),
            (zrow == 0, pltpu.roll(d, 1, 0)), (zrow == z - 1, pltpu.roll(d, rows - 1, 0)),
            (None, pltpu.roll(d, 1, 1)), (None, pltpu.roll(d, 127, 1)),
        )):
            w = (0.5 * scale) * (d + other)
            if outside is None:
                w_ref[i] = w
            else:
                w_ref[i] = jnp.where(outside, 0.0, w)
                w = jnp.where(outside, (0.5 * scale) * d, w)
            total = w if total is None else total + w
        return total

    def flat_around(w_ref, v, z):
        rows = v.shape[0]
        return (
            (w_ref[4] * pltpu.roll(v, 1, 1) + w_ref[5] * pltpu.roll(v, 127, 1))
            + ((w_ref[0] * pltpu.roll(v, z, 0) + w_ref[1] * pltpu.roll(v, rows - z, 0))
               + (w_ref[2] * pltpu.roll(v, 1, 0) + w_ref[3] * pltpu.roll(v, rows - 1, 0)))
        )

    def flat_coarse(v, slot):
        tmp3[slot] = v
        for z in range(z3):
            w = [
                tmp3[slot, pl.ds(x * z2 + 2 * z + i, bulks, stride=2 * z2), :]
                for x in range(2) for i in range(2)
            ]
            tmp4[slot, pl.ds(z, bulks, stride=z3), :] = (w[0] + w[1]) + (w[2] + w[3])
        return 0.125 * halved(tmp4[slot], even)

    def flat_fine(v):
        tmp4[3] = lanes_at(v, half)
        for z in range(z3):
            w = tmp4[3, pl.ds(z, bulks, stride=z3), :]
            for x in range(2):
                for i in range(2):
                    tmp3[3, pl.ds(x * z2 + 2 * z + i, bulks, stride=2 * z2), :] = w
        return tmp3[3]

    def sweeps(v, base, step, w_ref, z, count):
        rows = v.shape[0]

        def moved(a, reach):
            return {j: a if j == 0 else pltpu.roll(a, j % 128, 1) for j in range(-reach, reach + 1)}

        base = moved(base, count - 1)
        w = [moved(step * w_ref[i], count - 1) for i in range(6)]

        def run(v, many):
            v = moved(v, many)
            for left_over in range(many - 1, -1, -1):
                v = {
                    j: (rest * v[j] + base[j])
                    + ((w[4][j] * v[j + 1] + w[5][j] * v[j - 1])
                       + ((w[0][j] * pltpu.roll(v[j], z, 0) + w[1][j] * pltpu.roll(v[j], rows - z, 0))
                          + (w[2][j] * pltpu.roll(v[j], 1, 0) + w[3][j] * pltpu.roll(v[j], rows - 1, 0))))
                    for j in range(-left_over, left_over + 1)
                }
            return v[0]

        return run

    near1 = range(2, X1 - 2)

    def two(field, k):
        return field[2 * k - H], field[2 * k - H + 1]

    far = both_ways(0, (d0.at[H + 3], d_far.at[0]), (d0.at[H + cx - 4], d_far.at[1]))
    for copy, can, _ in far:
        go(copy, can)
    weights(d0_at, range(1, X0 - 1), *level0, face, 1.0)
    for k in near1:
        d1[k] = coarse_row(*two(d0, k), k)
    copies = both_ways(1, (d1.at[H : H + 2], d1.at[0:2]), (d1.at[H + 2 : H + 4], d1.at[X1 - 2 : X1]))
    for copy, can, _ in copies:
        go(copy, can)
    far += copies
    weights(lambda k: d1[k], near1[1:-1], *level1, face1, 0.25)
    face2 = face3 = None
    d2 = None

    for n in range(NEWTON):
        inner = range(1, X0 - 1)
        if n == 0:
            target, c_of = src, rb
        else:
            target, c_of = tgt, c0

            def reaction(x):
                sh, ch = sinh_cosh(pot[x])
                c0[x] = rb[x] * ch
                if x in inner:
                    tgt[x] = src[x] - rb[x] * sh
                    return True

            def misfit_row(x):
                tgt[x] = tgt[x] - face[x] * pot[x] + around(pot, x, *level0)

            for x in range(X0):
                reaction(x)
            for x in inner:
                misfit_row(x)
        for x in inner:
            st = safe_step(d0[x], face[x] + c_of[x])
            step0[x] = st
            v0[x] = st * target[x]
        if n == 0:
            beside = both_ways(3, (v0.at[H + 3], v_far.at[0]), (v0.at[H + cx - 4], v_far.at[1]))
            for copy, can, _ in beside:
                pl.when(can)(copy.start)
        for k in near1:
            c1[k] = coarse_row(*two(c_of, k), k)
        held = []
        if n == 0:
            held += beside
            copies = both_ways(2, (c1.at[H + 1], c1.at[1]), (c1.at[H + 2], c1.at[X1 - 2]))
            for copy, can, _ in copies:
                pl.when(can)(copy.start)
            far += copies
            held += copies

        def residual0(x):
            return rest * target[x] + around(v0, x, *level0)

        for k in near1[1:-1]:
            t1[k] = coarse_row(residual0(2 * k - H), residual0(2 * k - H + 1), X1 + k)
        for k in near1[1:-1]:
            st = safe_step(d1[k], face1[k] + c1[k])
            step1[k] = st
            v1[k] = st * t1[k]
        if n == 0:
            copies = both_ways(4, (v1.at[H], v1.at[0]), (v1.at[H + 3], v1.at[X1 - 1]))
            copies += both_ways(5, (t1.at[H + 1 : H + 3], t1.at[1:3]), (t1.at[H + 1 : H + 3], t1.at[X1 - 3 : X1 - 1]))
            beside += copies
        else:
            beside = copies = both_ways(6, (v1.at[H + 2], hv1.at[0]), (v1.at[H + 1], hv1.at[1]))
        for copy, can, _ in copies:
            pl.when(can)(copy.start)
        held += copies

        def residual1(k):
            return rest * t1[k, :, 0:128] + around(v1, k, *level1)[:, 0:128]

        t2_own = message(residual1, 0)
        c2_own = message(lambda k: c1[k, :, 0:128], 1)
        lane_m = iota((mrows, 128), 1)
        own, side, got, gots = (own0, side0, got0, gots0) if n == 0 else (own1, side1, got1, gots1)
        own[0:mrows] = jnp.where(lane_m < 64, t2_own, c2_own)
        to_high = jnp.where(lane_m < 64, c2_own, t2_own)
        to_low = to_high
        if n == 0:
            d2_own = message(lambda k: d1[k, :, 0:128], 2)
            own[mrows : 2 * mrows] = d2_own
            moved = pltpu.roll(d2_own, 32, 1)
            to_high = jnp.where(lane_m >> 5 == 2, moved, to_high)
            to_low = jnp.where(lane_m >> 5 == 3, moved, to_low)
        side[0], side[1] = to_high, to_low
        gather_send(n, own, side, got, gots)
        got[b] = own[...]
        if n == 0:
            for copy, _, can in far:
                pl.when(can)(copy.wait_recv)
            for x in (0, X0 - 1):
                weights(d0_at, range(x, x + 1), *level0, face, 1.0)
                st = safe_step(d0[x], face[x] + rb[x])
                step0[x] = st
                v0[x] = st * src[x]
            for rows in (range(1, 3), range(X1 - 3, X1 - 1)):
                weights(lambda k: d1[k], rows, *level1, face1, 0.25)
                for k in rows:
                    step1[k] = safe_step(d1[k], face1[k] + c1[k])
        gather_wait(n, got, gots)
        lane2 = iota((rows2, 128), 1)
        mine2, low2, high2 = [ref.reshape(rows2, 128) for ref in (got[:, 0:mrows], gots[0], gots[1])]
        t2 = jnp.where(lane2 < 64, mine2, jnp.where(lane2 < 96, high2, low2))
        c2 = pltpu.roll(jnp.where(lane2 >= 64, mine2, jnp.where(lane2 < 32, high2, low2)), 64, 1)
        if n == 0:
            d2 = jnp.where(
                lane2 < 64, got[:, mrows : 2 * mrows].reshape(rows2, 128),
                jnp.where(lane2 < 96, pltpu.roll(high2, 96, 1), pltpu.roll(low2, 32, 1)),
            )
            d3 = flat_coarse(d2, 2)
            face2 = flat_weights(w2, d2, z2, 0.25**2)
            face3 = flat_weights(w3, d3, z3, 0.25**3)
        step2 = safe_step(d2, face2 + c2)
        v2 = step2 * t2
        t3 = flat_coarse(rest * t2 + flat_around(w2, v2, z2), 0)
        c3 = flat_coarse(c2, 1)
        step3 = safe_step(d3, face3 + c3)
        v3 = step3 * t3
        run = sweeps(v3, v3, step3, w3, z3, ROUND)
        left_to_do = COARSE - 1
        while left_to_do:
            v3 = run(v3, min(ROUND, left_to_do))
            left_to_do -= min(ROUND, left_to_do)
        v2 = v2 + flat_fine(v3)
        v2 = (rest * v2 + step2 * t2) + step2 * flat_around(w2, v2, z2)
        v2_ref[0:mrows] = jnp.zeros((mrows, 128), f32)
        v2_ref[mrows : mrows + rows2] = v2
        v2_ref[mrows + rows2 :] = jnp.zeros((mrows, 128), f32)
        near = v2_ref[pl.ds(pl.multiple_of(b * mrows, 8), 3 * mrows), :]
        for i, index in enumerate((half, half_up)):
            wide = lanes_at(near, index)
            e_ref[i, pl.ds(0, 3 * mrows, stride=2), :] = wide
            e_ref[i, pl.ds(1, 3 * mrows, stride=2), :] = wide
        for copy, _, can in beside:
            pl.when(can)(copy.wait_recv)
        wide1 = range(X1) if n == 0 else near1
        wide0 = range(-1, X0 + 1) if n == 0 else range(H - 2, H + cx + 2)
        if n == 0:
            for k in (1, 2, X1 - 3, X1 - 2):
                v1[k] = step1[k] * t1[k]
        for k in wide1:
            before = v1[k]
            if n == 1 and k in (near1[0], near1[-1]):
                before = hv1[0 if k == near1[0] else 1]
            at = (k // 2) * z1
            tmp2[k] = before + jnp.concatenate([e_ref[i, at : at + z1, :] for i in range(2)], axis=1)
        for k in wide1[1:-1]:
            better = rest * tmp2[k] + step1[k] * (t1[k] + around(tmp2, k, *level1))
            fine = fine_row(better, k)
            for x in (2 * k - H, 2 * k - H + 1):
                if x in wide0:
                    vb[x + 1] = (v_far[0] if x < 0 else v_far[1] if x >= X0 else v0[x]) + fine
        for x in wide0[1:-1]:
            new = rest * vb[x + 1] + step0[x] * (target[x] + around(vb, x, *level0, shift=1))
            if n == 0:
                pot[x] = new
            else:
                pot2[x] = pot[x] + new
        for copy, can, _ in held:
            pl.when(can)(copy.wait_send)

    zrow = iota((z0, y), 0)
    end = (zrow == 0) | (zrow == z0 - 1)
    for x in range(H, H + cx):
        here = pot2[x]
        mid = here[:, 0:y]
        for i in range(2):
            turned[0, i, pl.ds(x - H, nz, stride=cx), :] = mid[:, i * 128 : (i + 1) * 128]
        sh, _ = sinh_cosh(mid)
        total = wx[x + 1, :, 0:y] * (mid - pot2[x + 1, :, 0:y]) + wx[x, :, 0:y] * (mid - pot2[x - 1, :, 0:y])
        total = total + wzp[x, :, 0:y] * (mid - pltpu.roll(mid, z0 - 1, 0)) + wzm[x, :, 0:y] * (mid - pltpu.roll(mid, 1, 0))
        total = total + wyp[x, :, 0:y] * (mid - pltpu.roll(here, W0 - 1, 1)[:, 0:y])
        total = total + wym[x, :, 0:y] * (mid - pltpu.roll(here, 1, 1)[:, 0:y])
        total = total + jnp.where(end, 0.5 * d0[x, :, 0:y], 0.0) * mid
        total = total + rb[x, :, 0:y] * sh - src[x, :, 0:y]
        for i in range(2):
            turned[1, i, pl.ds(x - H, nz, stride=cx), :] = total[:, i * 128 : (i + 1) * 128]
    for i in range(2):
        pot_out[:, i * 128 : (i + 1) * 128] = turned[0, i]
        mis_out[:, i * 128 : (i + 1) * 128] = turned[1, i]

    for out, _ in slab_copies:
        out.wait_send()
    for copy, can in sent:
        pl.when(can)(copy.wait_send)
    gather_drain(0, got0, gots0)
    gather_drain(1, got1, gots1)


def written(pot, mis, pot_out, mis_out, sem):
    copies = [pltpu.make_async_copy(pot, pot_out, sem.at[0]), pltpu.make_async_copy(mis, mis_out, sem.at[1])]
    for copy in copies:
        copy.start()
    for copy in copies:
        copy.wait()


def per_device(atom_counts, ion_flags, charge_cells, charge_values):
    slabs, bulks = lax.axis_size("slab"), lax.axis_size("bulk")
    nz, cx, y = ion_flags.shape
    z1, z2, z3 = nz // 2, nz // 4, nz // 8
    X0, X1 = cx + 2 * H, cx // 2 + 2 * H
    W0, W1 = y + 128, y // 2 + 128
    arows = nz * cx // slabs
    piece = 2 * arows + cx
    mrows = 2 * z2
    rows2, rows3 = bulks * mrows, bulks * z3
    i32 = jnp.int32
    vm = pltpu.VMEM
    dma = pltpu.SemaphoreType.DMA

    def level0(n=X0):
        return vm((n, nz, W0), f32)

    def level1(n=X1):
        return vm((n, z1, W1), f32)

    pot, mis = pl.pallas_call(
        lambda *refs: solver(slabs, bulks, nz, cx, y, *refs),
        out_shape=[jax.ShapeDtypeStruct((nz * cx, y), f32)] * 2,
        in_specs=[pl.BlockSpec(memory_space=pl.ANY)] * 4,
        out_specs=[pl.BlockSpec(memory_space=pltpu.VMEM)] * 2,
        scratch_shapes=[
            vm(atom_counts.shape, i32), vm((2, nz * cx, 128), i32),
            vm((1,) + charge_cells.shape, i32), vm((1,) + charge_values.shape, f32),
            vm((slabs, piece, 128), f32), vm((slabs, piece, 128), f32), vm((2, slabs, piece, 128), f32),
            level0(3 * cx), level0(), level0(),
            vm((2, 2, nz, 128), f32), vm((2, 2, nz, 128), f32), vm((2, 2, nz, 128), f32),
            level0(), level0(2), level0(), level0(X0 + 1), level0(), level0(), level0(), level0(), level0(), level0(),
            level0(), level0(), level0(2), level0(X0 + 2), level0(), level0(), level0(), vm((2 * X1, 3, nz, 128), f32),
            level1(), level1(X1 + 1), level1(), level1(), level1(), level1(), level1(), level1(), level1(), level1(),
            level1(), level1(2), vm((3, 2 * z1, 128), f32), level1(),
            vm((2 * mrows, 128), f32), vm((mrows, 128), f32), vm((2, mrows, 128), f32), vm((2, mrows, 128), f32),
            vm((bulks, 2 * mrows, 128), f32), vm((bulks, mrows, 128), f32),
            vm((2, bulks, mrows, 128), f32), vm((2, bulks, mrows, 128), f32),
            vm((6, rows2, 128), f32), vm((6, rows3, 128), f32),
            vm((rows2 + 2 * mrows, 128), f32), vm((2, 6 * mrows, 128), f32), vm((4, rows2, 128), f32), vm((4, rows3, 128), f32),
            vm((2, 2, nz * cx, 128), f32),
            dma((5,)), dma((slabs,)), dma((slabs,)), dma((slabs, 2)), dma((slabs, 2)),
            dma((3, 2)), dma((3, 2)), dma((2,)), dma((2,)),
            dma((7, 2)), dma((7, 2)), dma((2, 3)), dma((2, 3)),
        ],
        compiler_params=pltpu.CompilerParams(
            collective_id=0, has_side_effects=True, vmem_limit_bytes=40 << 20
        ),
    )(*[
        pltpu.with_memory_space_constraint(field, pltpu.HBM)
        for field in (atom_counts, ion_flags.reshape(nz * cx, y), charge_cells[None], charge_values[None])
    ])
    pot, mis = pl.pallas_call(
        written,
        out_shape=[jax.ShapeDtypeStruct((nz * cx, y), f32)] * 2,
        in_specs=[pl.BlockSpec(memory_space=pl.ANY)] * 2,
        out_specs=[pl.BlockSpec(memory_space=pl.ANY)] * 2,
        scratch_shapes=[dma((2,))],
        compiler_params=pltpu.CompilerParams(vmem_limit_bytes=1 << 20),
    )(pot, mis)
    return pot.reshape(nz, cx, y), mis.reshape(nz, cx, y)


def solution(mesh):
    placed = (
        P("slab", "bulk", None),
        P(None, "bulk", "slab"),
        P(("slab", "bulk")),
        P(("slab", "bulk")),
    )
    return jax.shard_map(
        per_device,
        mesh=mesh,
        in_specs=placed,
        out_specs=(P(None, "bulk", "slab"), P(None, "bulk", "slab")),
        check_vma=False,
    )
```

```python
import jax
import jax.numpy as jnp
import numpy as np
from jax import lax
from jax.experimental import pallas as pl
from jax.experimental.pallas import tpu as pltpu
from jax.sharding import PartitionSpec as P

COARSE = 8
NEWTON = 2
ROUND = 2
H = 4

taper_raw = np.exp(-0.5 * (np.arange(-4, 5) / 1.5) ** 2)
taper_weights = taper_raw / taper_raw.sum()
damping = 0.8
rest = 1.0 - damping
screening = 1.0
density_scale = 2.0

MESH_ID = pl.DeviceIdType.MESH
LN2 = float(np.log(2.0))
f32 = jnp.float32


def iota(shape, dim):
    return lax.broadcasted_iota(jnp.int32, shape, dim)


def log2(n):
    return int(n).bit_length() - 1


def mm(a, b):
    return lax.dot_general(
        a, b, (((1,), (0,)), ((), ())),
        precision=lax.Precision.HIGHEST, preferred_element_type=f32,
    )


def sinh_cosh(p):
    a, b = jnp.exp(p - LN2), jnp.exp(-p - LN2)
    q = jnp.minimum(p * p, 1.0)
    small = p * (
        1.0
        + q * (1 / 6) * (1.0 + q * (1 / 20) * (1.0 + q * (1 / 42) * (1.0 + q * (1 / 72) * (1.0 + q * (1 / 110)))))
    )
    return jnp.where(jnp.abs(p) < 1.0, small, a - b), a + b


def taper_y(density):
    width = density.shape[1]
    lane = iota(density.shape, 1)
    summed = float(taper_weights[4]) * density
    for k in range(1, 5):
        before = jnp.where(lane < k, 0.0, pltpu.roll(density, k, 1))
        after = jnp.where(lane >= width - k, 0.0, pltpu.roll(density, width - k, 1))
        summed = summed + float(taper_weights[4 + k]) * (before + after)
    return summed


def taper_z(rows, z, cx):
    i, j = iota((rows, rows), 0), iota((rows, rows), 1)
    far = jnp.abs((i & (z - 1)) - (j >> log2(cx)))
    band = jnp.zeros((rows, rows), f32)
    for k in range(5):
        band = jnp.where(far == k, float(taper_weights[4 + k]), band)
    return jnp.where((i >> log2(z)) == (j & (cx - 1)), band, 0.0)


def scattered(cells, values, rows, z, cx, y):
    entries = cells.shape[1]
    ly, lx = log2(y), log2(cx)
    row = ((cells >> ly) & (cx - 1)) * z + (cells >> (ly + lx))
    at_row = jnp.where(iota((rows, entries), 0) == row, values, 0.0)
    at_y = jnp.where(iota((y, entries), 0) == (cells & (y - 1)), f32(1.0), f32(0.0))
    return lax.dot_general(
        at_row, at_y, (((1,), (1,)), ((), ())),
        precision=lax.Precision.HIGHEST, preferred_element_type=f32,
    )


def lanes_at(v, index):
    parts = [
        jnp.take_along_axis(v[i : i + 8], index, axis=1, mode="promise_in_bounds")
        for i in range(0, v.shape[0], 8)
    ]
    return parts[0] if len(parts) == 1 else jnp.concatenate(parts, axis=0)


def halved(v, index):
    return lanes_at(v + pltpu.roll(v, 127, 1), index)


def solver(
    slabs, bulks, nz, cx, y,
    atoms_hbm, flags_hbm, cells_hbm, values_hbm, pot_out, mis_out,
    atoms_in, flags_in, cells_in, values_in,
    ay, abuf, nbuf, dens, opened, src, yout, yin, ycorner,
    d0, d_far, rb, wx, wyp, wym, wzp, wzm, face, c0, step0, v0, v_far, vb, tgt, pot, pot2, tmp,
    d1, w1x, w1yp, w1ym, w1zp, w1zm, face1, c1, step1, t1, v1, hv1, tmp1, tmp2,
    own0, own1, side0, side1, got0, got1, gots0, gots1, w2, w3, v2_ref, e_ref, tmp3, tmp4, turned,
    load_sem, a_send, a_recv, f_send, f_recv, x_send, x_recv, y_send, y_recv,
    e_send, e_recv, g_send, g_recv,
):
    s, b = lax.axis_index("slab"), lax.axis_index("bulk")
    z0, z1, z2, z3 = nz, nz // 2, nz // 4, nz // 8
    X0, X1 = cx + 2 * H, cx // 2 + 2 * H
    W0, W1 = y + 128, y // 2 + 128
    mrows = 2 * z2
    rows2, rows3 = bulks * mrows, bulks * z3
    at_left, at_right = b == 0, b == bulks - 1
    at_low, at_high = s == 0, s == slabs - 1
    has_left, has_right = b > 0, b < bulks - 1
    has_low, has_high = s > 0, s < slabs - 1

    loads = [
        pltpu.make_async_copy(there, here, load_sem.at[i])
        for i, (there, here) in enumerate((
            (atoms_hbm, atoms_in), (cells_hbm, cells_in), (values_hbm, values_in),
            (flags_hbm.at[:, 0:128], flags_in.at[0]), (flags_hbm.at[:, 128:256], flags_in.at[1]),
        ))
    ]
    for load in loads:
        load.start()

    def flip(at, k):
        for i in range(log2(k) + 1):
            if k >> i & 1:
                at = at + (1 << i) * (1 - 2 * (at // (1 << i) % 2))
        return at

    barrier = pltpu.get_barrier_semaphore()
    for k in range(1, slabs):
        pl.semaphore_signal(barrier, inc=1, device_id=(flip(s, k), b), device_id_type=MESH_ID)
    for k in range(1, bulks):
        pl.semaphore_signal(barrier, inc=1, device_id=(s, flip(b, k)), device_id_type=MESH_ID)

    def clear(*refs):
        for ref in refs:
            ref[...] = jnp.zeros(ref.shape, ref.dtype)

    @pl.when(at_left)
    def _():
        clear(nbuf.at[0], opened.at[0:H], src.at[0:H], ycorner.at[0], hv1.at[0], d_far.at[0], v_far.at[0],
              d1.at[0:2], c1.at[1], t1.at[1:3], v1.at[0])

    @pl.when(at_right)
    def _():
        clear(
            nbuf.at[1], opened.at[H + cx : X0], src.at[H + cx : X0], ycorner.at[1],
            hv1.at[1], d_far.at[1], v_far.at[1], d1.at[X1 - 2 : X1], c1.at[X1 - 2], t1.at[X1 - 3 : X1 - 1], v1.at[X1 - 1],
        )

    @pl.when(at_low)
    def _():
        clear(gots0.at[0], gots1.at[0], yin.at[0])

    @pl.when(at_high)
    def _():
        clear(gots0.at[1], gots1.at[1], yin.at[1])

    def remote(source, target, send, recv, to):
        return pltpu.make_async_remote_copy(
            src_ref=source, dst_ref=target, send_sem=send, recv_sem=recv,
            device_id=to, device_id_type=MESH_ID,
        )

    right, left = (s, b + 1), (s, b - 1)
    high, low = (s + 1, b), (s - 1, b)
    sent = []

    def go(copy, can):
        pl.when(can)(copy.start)
        sent.append((copy, can))

    loads[0].wait()
    smooth_y = taper_y(atoms_in[...].astype(f32).reshape(-1, slabs * y))
    arows = smooth_y.shape[0]
    planes = arows // cx
    lane_a = iota((arows, 128), 1)
    lane_c = iota((cx, 128), 1)
    nothing = jnp.zeros((arows, 128), f32)
    for t in range(slabs):
        for i in range(2):
            ay[t, i * arows : (i + 1) * arows] = smooth_y[:, t * y + i * 128 : t * y + (i + 1) * 128]
        after = smooth_y[:, (t + 1) * y : (t + 1) * y + 128] if t < slabs - 1 else nothing
        before = smooth_y[:, t * y - 128 : t * y] if t else nothing
        beside = jnp.where(lane_a < 64, after, before)
        packed = beside[0:cx]
        for g in range(1, planes):
            moved = pltpu.roll(beside[g * cx : (g + 1) * cx], 32 * g, 1)
            packed = jnp.where((((lane_c + 16) >> 5) & 3) == g, moved, packed)
        ay[t, 2 * arows :] = packed

    slab_copies = [
        (remote(ay.at[flip(s, k)], abuf.at[s], a_send.at[k], a_recv.at[k], (flip(s, k), b)),
         remote(ay.at[flip(s, k)], abuf.at[flip(s, k)], a_send.at[k], a_recv.at[k], (flip(s, k), b)))
        for k in range(1, slabs)
    ]
    pl.semaphore_wait(barrier, slabs + bulks - 2)
    for out, _ in slab_copies:
        out.start()

    def pass_on(k):
        which = flip(s, k) if k else s
        return [
            (remote(abuf.at[which], nbuf.at[0, which], f_send.at[k, 0], f_recv.at[k, 0], right), has_right, has_left),
            (remote(abuf.at[which], nbuf.at[1, which], f_send.at[k, 1], f_recv.at[k, 1], left), has_left, has_right),
        ]

    passed = []
    abuf[s] = ay[s]
    passed += pass_on(0)
    for copy, can, _ in passed:
        go(copy, can)

    def rows_both_ways(source, target, slot, lanes):
        return [
            (remote(
                source.at[cx : cx + H, :, lanes], target.at[0:H, :, lanes],
                x_send.at[slot, 0], x_recv.at[slot, 0], right,
            ), has_right, has_left),
            (remote(
                source.at[H : 2 * H, :, lanes], target.at[H + cx : X0, :, lanes],
                x_send.at[slot, 1], x_recv.at[slot, 1], left,
            ), has_left, has_right),
        ]

    for load in loads[1:]:
        load.wait()
    for x in range(cx):
        for i in range(2):
            flags = flags_in[i, pl.ds(x, nz, stride=cx), :]
            opened[H + x, :, i * 128 : (i + 1) * 128] = 1.0 - flags.astype(f32)
    x_copies = rows_both_ways(opened, opened, 0, slice(0, y))
    for copy, can, _ in x_copies:
        go(copy, can)
    charges = scattered(cells_in[...], values_in[...], cx * z0, z0, cx, y)
    for x in range(cx):
        src[H + x, :, 0:y] = charges[x * z0 : (x + 1) * z0]
    copies = rows_both_ways(src, src, 1, slice(0, y))
    for copy, can, _ in copies:
        go(copy, can)
    x_copies += copies

    lane_h = iota((z0, 128), 1)
    for q in range(2):
        to_high = to_low = jnp.zeros((z0, 128), f32)
        for j in range(8):
            field = (opened, src)[j // 4]
            x = H + 4 * q + j % 4
            to_high = jnp.where(lane_h >> 4 == j, pltpu.roll(field[x, :, y - 128 : y], (16 * j + 16) % 128, 1), to_high)
            to_low = jnp.where(lane_h >> 4 == (j + 1) % 8, pltpu.roll(field[x, :, 0:128], (16 * j + 16) % 128, 1), to_low)
        yout[0, q], yout[1, q] = to_high, to_low
    y_copies = [
        (remote(yout.at[0], yin.at[0], y_send.at[0], y_recv.at[0], high), has_high, has_low),
        (remote(yout.at[1], yin.at[1], y_send.at[1], y_recv.at[1], low), has_low, has_high),
    ]
    for copy, can, _ in y_copies:
        go(copy, can)
    corner_copies = [
        (remote(yin.at[:, 1], ycorner.at[0], x_send.at[2, 0], x_recv.at[2, 0], right), has_right, has_left),
        (remote(yin.at[:, 0], ycorner.at[1], x_send.at[2, 1], x_recv.at[2, 1], left), has_left, has_right),
    ]

    along_z = taper_z(cx * z0, z0, cx)
    for k in range(1, slabs):
        slab_copies[k - 1][1].wait_recv()
        copies = pass_on(k)
        for copy, can, _ in copies:
            go(copy, can)
        passed += copies

    def smooth_z(pieces, at):
        columns = [pieces[:, i * arows : (i + 1) * arows].reshape(cx * z0, 128) for i in range(2)]
        edges = []
        for t in range(slabs):
            packed = pieces[t, 2 * arows :]
            edges += [packed] + [pltpu.roll(packed, 128 - 32 * g, 1) for g in range(1, planes)]
        columns.append(jnp.concatenate(edges, axis=0))
        for i, column in enumerate(columns):
            dens[at : at + cx, :, i * 128 : (i + 1) * 128] = mm(along_z, column).reshape(cx, z0, 128)

    for copy, _, can in y_copies:
        pl.when(can)(copy.wait_recv)
    for copy, can, _ in corner_copies:
        go(copy, can)
    smooth_z(abuf, cx)

    def unpack(x, from_low, from_high):
        for a, field in enumerate((opened, src)):
            j = 4 * a + x % 4
            both = jnp.where(lane_h >> 4 == j, from_low, from_high)
            both = pltpu.roll(both, (112 - 16 * j) % 128, 1)
            field[x, :, y:W0] = jnp.where((lane_h < 16) | (lane_h >= 112), both, 0.0)

    for x in range(H, H + cx):
        unpack(x, yin[0, x // 4 - 1], yin[1, x // 4 - 1])
    lane0 = iota((z0, W0), 1)
    keep_low = jnp.where(at_low, f32(0.0), f32(1.0))
    keep_high = jnp.where(at_high, f32(0.0), f32(1.0))
    keep_y = jnp.where(lane0 < y, 1.0, jnp.where(lane0 < y + 64, keep_high, keep_low))
    keep_left = jnp.where(at_left, f32(0.0), f32(1.0))
    keep_right = jnp.where(at_right, f32(0.0), f32(1.0))
    zrow0 = iota((z0, W0), 0)
    lane128 = iota((8, 128), 1)
    even = (2 * lane128) & 127
    half = lane128 >> 1
    half_up = 64 + half
    half_split = jnp.where(lane128 < 64, half, half_up)

    for copy, _, can in x_copies + corner_copies:
        pl.when(can)(copy.wait_recv)
    for x in range(H):
        unpack(x, ycorner[0, 0], ycorner[0, 1])
        unpack(H + cx + x, ycorner[1, 0], ycorner[1, 1])
    for copy, _, can in passed:
        pl.when(can)(copy.wait_recv)
    smooth_z(nbuf.at[0], 0)
    smooth_z(nbuf.at[1], 2 * cx)
    for x in range(X0):
        smoothed = float(taper_weights[4]) * dens[x + 4]
        for k in range(1, 5):
            smoothed = smoothed + float(taper_weights[4 + k]) * (dens[x + 4 - k] + dens[x + 4 + k])
        shading = jnp.exp(-smoothed / density_scale)
        keep = keep_y
        if x < H:
            keep = keep_y * keep_left
        elif x >= H + cx:
            keep = keep_y * keep_right
        d0[x] = keep * (2.0 + 78.0 * shading)
        rb[x] = screening * shading * shading * opened[x]

    def weights(at, rows, wx, wyp, wym, wzp, wzm, face, scale):
        for x in rows:
            v = at(x)
            z, w = v.shape
            zrow = iota((z, w), 0)
            if x == rows[0]:
                wx[x] = (0.5 * scale) * (at(x - 1) + v)
            wx[x + 1] = (0.5 * scale) * (v + at(x + 1))
            yp = (0.5 * scale) * (v + pltpu.roll(v, w - 1, 1))
            ym = (0.5 * scale) * (v + pltpu.roll(v, 1, 1))
            zp = jnp.where(zrow == z - 1, 0.0, (0.5 * scale) * (v + pltpu.roll(v, z - 1, 0)))
            zm = jnp.where(zrow == 0, 0.0, (0.5 * scale) * (v + pltpu.roll(v, 1, 0)))
            wyp[x], wym[x], wzp[x], wzm[x] = yp, ym, zp, zm
            ends = jnp.where((zrow == 0) | (zrow == z - 1), (0.5 * scale) * v, 0.0)
            face[x] = wx[x] + wx[x + 1] + yp + ym + zp + zm + ends

    def around(v, x, wx, wyp, wym, wzp, wzm, shift=0):
        here = v[x + shift]
        z, w = here.shape
        return (
            (wx[x + 1] * v[x + shift + 1] + wx[x] * v[x + shift - 1])
            + (wzp[x] * pltpu.roll(here, z - 1, 0) + wzm[x] * pltpu.roll(here, 1, 0))
            + (wyp[x] * pltpu.roll(here, w - 1, 1) + wym[x] * pltpu.roll(here, 1, 1))
        )

    def d0_at(x):
        return d_far[0] if x < 0 else d_far[1] if x >= X0 else d0[x]

    def both_ways(slot, to_right, to_left):
        return [
            (remote(to_right[0], to_right[1], e_send.at[slot, 0], e_recv.at[slot, 0], right), has_right, has_left),
            (remote(to_left[0], to_left[1], e_send.at[slot, 1], e_recv.at[slot, 1], left), has_left, has_right),
        ]

    level0 = (wx, wyp, wym, wzp, wzm)
    level1 = (w1x, w1yp, w1ym, w1zp, w1zm)

    def coarse_row(a, c, slot):
        both = a + c
        lane = iota((z1, 128), 1)
        parts = []
        for i in range(3):
            tmp[slot, i] = both[:, i * 128 : (i + 1) * 128]
            parts.append(halved(
                tmp[slot, i, pl.ds(0, z1, stride=2), :] + tmp[slot, i, pl.ds(1, z1, stride=2), :], even
            ))
        return 0.125 * jnp.concatenate([jnp.where(lane < 64, parts[0], parts[1]), parts[2]], axis=1)

    def fine_row(c, slot):
        for i, index in enumerate((half, half_up, half_split)):
            wide = lanes_at(c[:, 128 * (i // 2) : 128 * (i // 2) + 128], index)
            tmp[slot, i, pl.ds(0, z1, stride=2), :] = wide
            tmp[slot, i, pl.ds(1, z1, stride=2), :] = wide
        return jnp.concatenate([tmp[slot, i] for i in range(3)], axis=1)

    def message(f, slot):
        for k in range(2):
            tmp1[slot, k * z1 : (k + 1) * z1, :] = f(H + 2 * k) + f(H + 2 * k + 1)
        w = tmp1[slot, pl.ds(0, mrows, stride=2), :] + tmp1[slot, pl.ds(1, mrows, stride=2), :]
        return 0.125 * halved(w, even)

    def safe_step(d, diagonal):
        return jnp.where(d > 0.0, damping / diagonal, 0.0)

    def gather_send(n, own, side, got, gots):
        for k in range(bulks - 1, 0, -1):
            remote(own, got.at[b], g_send.at[n, 2], g_recv.at[n, 2], (s, flip(b, k))).start()
        for i, (can, row) in enumerate(((has_high, s + 1), (has_low, s - 1))):
            @pl.when(can)
            def _():
                for k in range(bulks - 1, -1, -1):
                    remote(
                        side.at[i], gots.at[i, b], g_send.at[n, i], g_recv.at[n, i],
                        (row, flip(b, k) if k else b),
                    ).start()

    def gather_copy(n, got, gots, i):
        part = got.at[0 : bulks - 1] if i == 2 else gots.at[i]
        return remote(part, part, g_send.at[n, i], g_recv.at[n, i], (s, flip(b, 1)))

    def gather_wait(n, got, gots):
        gather_copy(n, got, gots, 2).wait_recv()
        pl.when(has_low)(gather_copy(n, got, gots, 0).wait_recv)
        pl.when(has_high)(gather_copy(n, got, gots, 1).wait_recv)

    def gather_drain(n, got, gots):
        gather_copy(n, got, gots, 2).wait_send()
        pl.when(has_high)(gather_copy(n, got, gots, 0).wait_send)
        pl.when(has_low)(gather_copy(n, got, gots, 1).wait_send)

    def flat_weights(w_ref, d, z, scale):
        rows = d.shape[0]
        row = iota(d.shape, 0)
        zrow = row & (z - 1)
        total = None
        for i, (outside, other) in enumerate((
            (row < z, pltpu.roll(d, z, 0)), (row >= rows - z, pltpu.roll(d, rows - z, 0)),
            (zrow == 0, pltpu.roll(d, 1, 0)), (zrow == z - 1, pltpu.roll(d, rows - 1, 0)),
            (None, pltpu.roll(d, 1, 1)), (None, pltpu.roll(d, 127, 1)),
        )):
            w = (0.5 * scale) * (d + other)
            if outside is None:
                w_ref[i] = w
            else:
                w_ref[i] = jnp.where(outside, 0.0, w)
                w = jnp.where(outside, (0.5 * scale) * d, w)
            total = w if total is None else total + w
        return total

    def flat_around(w_ref, v, z):
        rows = v.shape[0]
        return (
            (w_ref[4] * pltpu.roll(v, 1, 1) + w_ref[5] * pltpu.roll(v, 127, 1))
            + ((w_ref[0] * pltpu.roll(v, z, 0) + w_ref[1] * pltpu.roll(v, rows - z, 0))
               + (w_ref[2] * pltpu.roll(v, 1, 0) + w_ref[3] * pltpu.roll(v, rows - 1, 0)))
        )

    def flat_coarse(v, slot):
        tmp3[slot] = v
        for z in range(z3):
            w = [
                tmp3[slot, pl.ds(x * z2 + 2 * z + i, bulks, stride=2 * z2), :]
                for x in range(2) for i in range(2)
            ]
            tmp4[slot, pl.ds(z, bulks, stride=z3), :] = (w[0] + w[1]) + (w[2] + w[3])
        return 0.125 * halved(tmp4[slot], even)

    def flat_fine(v):
        tmp4[3] = lanes_at(v, half)
        for z in range(z3):
            w = tmp4[3, pl.ds(z, bulks, stride=z3), :]
            for x in range(2):
                for i in range(2):
                    tmp3[3, pl.ds(x * z2 + 2 * z + i, bulks, stride=2 * z2), :] = w
        return tmp3[3]

    def sweeps(v, base, step, w_ref, z, count):
        rows = v.shape[0]

        def moved(a, reach):
            return {j: a if j == 0 else pltpu.roll(a, j % 128, 1) for j in range(-reach, reach + 1)}

        base = moved(base, count - 1)
        w = [moved(step * w_ref[i], count - 1) for i in range(6)]

        def run(v, many):
            v = moved(v, many)
            for left_over in range(many - 1, -1, -1):
                v = {
                    j: (rest * v[j] + base[j])
                    + ((w[4][j] * v[j + 1] + w[5][j] * v[j - 1])
                       + ((w[0][j] * pltpu.roll(v[j], z, 0) + w[1][j] * pltpu.roll(v[j], rows - z, 0))
                          + (w[2][j] * pltpu.roll(v[j], 1, 0) + w[3][j] * pltpu.roll(v[j], rows - 1, 0))))
                    for j in range(-left_over, left_over + 1)
                }
            return v[0]

        return run

    near1 = range(2, X1 - 2)

    def two(field, k):
        return field[2 * k - H], field[2 * k - H + 1]

    far = both_ways(0, (d0.at[H + 3], d_far.at[0]), (d0.at[H + cx - 4], d_far.at[1]))
    for copy, can, _ in far:
        go(copy, can)
    weights(d0_at, range(1, X0 - 1), *level0, face, 1.0)
    for k in near1:
        d1[k] = coarse_row(*two(d0, k), k)
    copies = both_ways(1, (d1.at[H : H + 2], d1.at[0:2]), (d1.at[H + 2 : H + 4], d1.at[X1 - 2 : X1]))
    for copy, can, _ in copies:
        go(copy, can)
    far += copies
    weights(lambda k: d1[k], near1[1:-1], *level1, face1, 0.25)
    face2 = face3 = None
    d2 = None

    for n in range(NEWTON):
        inner = range(1, X0 - 1)
        if n == 0:
            target, c_of = src, rb
        else:
            target, c_of = tgt, c0

            def reaction(x):
                sh, ch = sinh_cosh(pot[x])
                c0[x] = rb[x] * ch
                if x in inner:
                    tgt[x] = src[x] - rb[x] * sh
                    return True

            def misfit_row(x):
                tgt[x] = tgt[x] - face[x] * pot[x] + around(pot, x, *level0)

            for x in range(X0):
                reaction(x)
            for x in inner:
                misfit_row(x)
        for x in inner:
            st = safe_step(d0[x], face[x] + c_of[x])
            step0[x] = st
            v0[x] = st * target[x]
        if n == 0:
            beside = both_ways(3, (v0.at[H + 3], v_far.at[0]), (v0.at[H + cx - 4], v_far.at[1]))
        for k in near1:
            c1[k] = coarse_row(*two(c_of, k), k)
        held = []
        if n == 0:
            held += beside
            copies = both_ways(2, (c1.at[H + 1], c1.at[1]), (c1.at[H + 2], c1.at[X1 - 2]))
            for copy, can, _ in copies:
                pl.when(can)(copy.start)
            far += copies
            held += copies

        def residual0(x):
            return rest * target[x] + around(v0, x, *level0)

        for k in near1[1:-1]:
            t1[k] = coarse_row(residual0(2 * k - H), residual0(2 * k - H + 1), X1 + k)
        for k in near1[1:-1]:
            st = safe_step(d1[k], face1[k] + c1[k])
            step1[k] = st
            v1[k] = st * t1[k]
        if n == 0:
            copies = both_ways(4, (v1.at[H], v1.at[0]), (v1.at[H + 3], v1.at[X1 - 1]))
            copies += both_ways(5, (t1.at[H + 1 : H + 3], t1.at[1:3]), (t1.at[H + 1 : H + 3], t1.at[X1 - 3 : X1 - 1]))
            beside += copies
        else:
            beside = copies = both_ways(6, (v1.at[H + 2], hv1.at[0]), (v1.at[H + 1], hv1.at[1]))
        late = copies
        held += copies

        def residual1(k):
            return rest * t1[k, :, 0:128] + around(v1, k, *level1)[:, 0:128]

        t2_own = message(residual1, 0)
        c2_own = message(lambda k: c1[k, :, 0:128], 1)
        lane_m = iota((mrows, 128), 1)
        own, side, got, gots = (own0, side0, got0, gots0) if n == 0 else (own1, side1, got1, gots1)
        own[0:mrows] = jnp.where(lane_m < 64, t2_own, c2_own)
        to_high = jnp.where(lane_m < 64, c2_own, t2_own)
        to_low = to_high
        if n == 0:
            d2_own = message(lambda k: d1[k, :, 0:128], 2)
            own[mrows : 2 * mrows] = d2_own
            moved = pltpu.roll(d2_own, 32, 1)
            to_high = jnp.where(lane_m >> 5 == 2, moved, to_high)
            to_low = jnp.where(lane_m >> 5 == 3, moved, to_low)
        side[0], side[1] = to_high, to_low
        gather_send(n, own, side, got, gots)
        for copy, can, _ in late + (beside[:2] if n == 0 else []):
            pl.when(can)(copy.start)
        got[b] = own[...]
        if n == 0:
            for copy, _, can in far:
                pl.when(can)(copy.wait_recv)
            for x in (0, X0 - 1):
                weights(d0_at, range(x, x + 1), *level0, face, 1.0)
                st = safe_step(d0[x], face[x] + rb[x])
                step0[x] = st
                v0[x] = st * src[x]
            for rows in (range(1, 3), range(X1 - 3, X1 - 1)):
                weights(lambda k: d1[k], rows, *level1, face1, 0.25)
                for k in rows:
                    step1[k] = safe_step(d1[k], face1[k] + c1[k])
        gather_wait(n, got, gots)
        lane2 = iota((rows2, 128), 1)
        mine2, low2, high2 = [ref.reshape(rows2, 128) for ref in (got[:, 0:mrows], gots[0], gots[1])]
        t2 = jnp.where(lane2 < 64, mine2, jnp.where(lane2 < 96, high2, low2))
        c2 = pltpu.roll(jnp.where(lane2 >= 64, mine2, jnp.where(lane2 < 32, high2, low2)), 64, 1)
        if n == 0:
            d2 = jnp.where(
                lane2 < 64, got[:, mrows : 2 * mrows].reshape(rows2, 128),
                jnp.where(lane2 < 96, pltpu.roll(high2, 96, 1), pltpu.roll(low2, 32, 1)),
            )
            d3 = flat_coarse(d2, 2)
            face2 = flat_weights(w2, d2, z2, 0.25**2)
            face3 = flat_weights(w3, d3, z3, 0.25**3)
        step2 = safe_step(d2, face2 + c2)
        v2 = step2 * t2
        t3 = flat_coarse(rest * t2 + flat_around(w2, v2, z2), 0)
        c3 = flat_coarse(c2, 1)
        step3 = safe_step(d3, face3 + c3)
        v3 = step3 * t3
        run = sweeps(v3, v3, step3, w3, z3, ROUND)
        left_to_do = COARSE - 1
        while left_to_do:
            v3 = run(v3, min(ROUND, left_to_do))
            left_to_do -= min(ROUND, left_to_do)
        v2 = v2 + flat_fine(v3)
        v2 = (rest * v2 + step2 * t2) + step2 * flat_around(w2, v2, z2)
        v2_ref[0:mrows] = jnp.zeros((mrows, 128), f32)
        v2_ref[mrows : mrows + rows2] = v2
        v2_ref[mrows + rows2 :] = jnp.zeros((mrows, 128), f32)
        near = v2_ref[pl.ds(pl.multiple_of(b * mrows, 8), 3 * mrows), :]
        for i, index in enumerate((half, half_up)):
            wide = lanes_at(near, index)
            e_ref[i, pl.ds(0, 3 * mrows, stride=2), :] = wide
            e_ref[i, pl.ds(1, 3 * mrows, stride=2), :] = wide
        for copy, _, can in beside:
            pl.when(can)(copy.wait_recv)
        wide1 = range(X1) if n == 0 else near1
        wide0 = range(-1, X0 + 1) if n == 0 else range(H - 2, H + cx + 2)
        if n == 0:
            for k in (1, 2, X1 - 3, X1 - 2):
                v1[k] = step1[k] * t1[k]
        for k in wide1:
            before = v1[k]
            if n == 1 and k in (near1[0], near1[-1]):
                before = hv1[0 if k == near1[0] else 1]
            at = (k // 2) * z1
            tmp2[k] = before + jnp.concatenate([e_ref[i, at : at + z1, :] for i in range(2)], axis=1)
        for k in wide1[1:-1]:
            better = rest * tmp2[k] + step1[k] * (t1[k] + around(tmp2, k, *level1))
            fine = fine_row(better, k)
            for x in (2 * k - H, 2 * k - H + 1):
                if x in wide0:
                    vb[x + 1] = (v_far[0] if x < 0 else v_far[1] if x >= X0 else v0[x]) + fine
        for x in wide0[1:-1]:
            new = rest * vb[x + 1] + step0[x] * (target[x] + around(vb, x, *level0, shift=1))
            if n == 0:
                pot[x] = new
            else:
                pot2[x] = pot[x] + new
        for copy, can, _ in held:
            pl.when(can)(copy.wait_send)

    zrow = iota((z0, y), 0)
    end = (zrow == 0) | (zrow == z0 - 1)
    for x in range(H, H + cx):
        here = pot2[x]
        mid = here[:, 0:y]
        for i in range(2):
            turned[0, i, pl.ds(x - H, nz, stride=cx), :] = mid[:, i * 128 : (i + 1) * 128]
        sh, _ = sinh_cosh(mid)
        total = wx[x + 1, :, 0:y] * (mid - pot2[x + 1, :, 0:y]) + wx[x, :, 0:y] * (mid - pot2[x - 1, :, 0:y])
        total = total + wzp[x, :, 0:y] * (mid - pltpu.roll(mid, z0 - 1, 0)) + wzm[x, :, 0:y] * (mid - pltpu.roll(mid, 1, 0))
        total = total + wyp[x, :, 0:y] * (mid - pltpu.roll(here, W0 - 1, 1)[:, 0:y])
        total = total + wym[x, :, 0:y] * (mid - pltpu.roll(here, 1, 1)[:, 0:y])
        total = total + jnp.where(end, 0.5 * d0[x, :, 0:y], 0.0) * mid
        total = total + rb[x, :, 0:y] * sh - src[x, :, 0:y]
        for i in range(2):
            turned[1, i, pl.ds(x - H, nz, stride=cx), :] = total[:, i * 128 : (i + 1) * 128]
    for i in range(2):
        pot_out[:, i * 128 : (i + 1) * 128] = turned[0, i]
        mis_out[:, i * 128 : (i + 1) * 128] = turned[1, i]

    for out, _ in slab_copies:
        out.wait_send()
    for copy, can in sent:
        pl.when(can)(copy.wait_send)
    gather_drain(0, got0, gots0)
    gather_drain(1, got1, gots1)


def written(pot, mis, pot_out, mis_out, sem):
    copies = [pltpu.make_async_copy(pot, pot_out, sem.at[0]), pltpu.make_async_copy(mis, mis_out, sem.at[1])]
    for copy in copies:
        copy.start()
    for copy in copies:
        copy.wait()


def per_device(atom_counts, ion_flags, charge_cells, charge_values):
    slabs, bulks = lax.axis_size("slab"), lax.axis_size("bulk")
    nz, cx, y = ion_flags.shape
    z1, z2, z3 = nz // 2, nz // 4, nz // 8
    X0, X1 = cx + 2 * H, cx // 2 + 2 * H
    W0, W1 = y + 128, y // 2 + 128
    arows = nz * cx // slabs
    piece = 2 * arows + cx
    mrows = 2 * z2
    rows2, rows3 = bulks * mrows, bulks * z3
    i32 = jnp.int32
    vm = pltpu.VMEM
    dma = pltpu.SemaphoreType.DMA

    def level0(n=X0):
        return vm((n, nz, W0), f32)

    def level1(n=X1):
        return vm((n, z1, W1), f32)

    pot, mis = pl.pallas_call(
        lambda *refs: solver(slabs, bulks, nz, cx, y, *refs),
        out_shape=[jax.ShapeDtypeStruct((nz * cx, y), f32)] * 2,
        in_specs=[pl.BlockSpec(memory_space=pl.ANY)] * 4,
        out_specs=[pl.BlockSpec(memory_space=pltpu.VMEM)] * 2,
        scratch_shapes=[
            vm(atom_counts.shape, i32), vm((2, nz * cx, 128), i32),
            vm((1,) + charge_cells.shape, i32), vm((1,) + charge_values.shape, f32),
            vm((slabs, piece, 128), f32), vm((slabs, piece, 128), f32), vm((2, slabs, piece, 128), f32),
            level0(3 * cx), level0(), level0(),
            vm((2, 2, nz, 128), f32), vm((2, 2, nz, 128), f32), vm((2, 2, nz, 128), f32),
            level0(), level0(2), level0(), level0(X0 + 1), level0(), level0(), level0(), level0(), level0(), level0(),
            level0(), level0(), level0(2), level0(X0 + 2), level0(), level0(), level0(), vm((2 * X1, 3, nz, 128), f32),
            level1(), level1(X1 + 1), level1(), level1(), level1(), level1(), level1(), level1(), level1(), level1(),
            level1(), level1(2), vm((3, 2 * z1, 128), f32), level1(),
            vm((2 * mrows, 128), f32), vm((mrows, 128), f32), vm((2, mrows, 128), f32), vm((2, mrows, 128), f32),
            vm((bulks, 2 * mrows, 128), f32), vm((bulks, mrows, 128), f32),
            vm((2, bulks, mrows, 128), f32), vm((2, bulks, mrows, 128), f32),
            vm((6, rows2, 128), f32), vm((6, rows3, 128), f32),
            vm((rows2 + 2 * mrows, 128), f32), vm((2, 6 * mrows, 128), f32), vm((4, rows2, 128), f32), vm((4, rows3, 128), f32),
            vm((2, 2, nz * cx, 128), f32),
            dma((5,)), dma((slabs,)), dma((slabs,)), dma((slabs, 2)), dma((slabs, 2)),
            dma((3, 2)), dma((3, 2)), dma((2,)), dma((2,)),
            dma((7, 2)), dma((7, 2)), dma((2, 3)), dma((2, 3)),
        ],
        compiler_params=pltpu.CompilerParams(
            collective_id=0, has_side_effects=True, vmem_limit_bytes=40 << 20
        ),
    )(*[
        pltpu.with_memory_space_constraint(field, pltpu.HBM)
        for field in (atom_counts, ion_flags.reshape(nz * cx, y), charge_cells[None], charge_values[None])
    ])
    pot, mis = pl.pallas_call(
        written,
        out_shape=[jax.ShapeDtypeStruct((nz * cx, y), f32)] * 2,
        in_specs=[pl.BlockSpec(memory_space=pl.ANY)] * 2,
        out_specs=[pl.BlockSpec(memory_space=pl.ANY)] * 2,
        scratch_shapes=[dma((2,))],
        compiler_params=pltpu.CompilerParams(vmem_limit_bytes=1 << 20),
    )(pot, mis)
    return pot.reshape(nz, cx, y), mis.reshape(nz, cx, y)


def solution(mesh):
    placed = (
        P("slab", "bulk", None),
        P(None, "bulk", "slab"),
        P(("slab", "bulk")),
        P(("slab", "bulk")),
    )
    return jax.shard_map(
        per_device,
        mesh=mesh,
        in_specs=placed,
        out_specs=(P(None, "bulk", "slab"), P(None, "bulk", "slab")),
        check_vma=False,
    )
```
